128 devices in a mesh: expert: 32 (over z, x, core), dp: 4 (over y).
Axes of the slice: x: 4, y: 4, z: 4, core: 2. Of those that a mesh axis runs over, the one named last changes fastest.
Arguments:
- tokens: bfloat16 [8192, 2048], P(('expert', 'dp')), may hold values from -6 to 6
- routes: int32 [8192, 8], P(('expert', 'dp')), may hold values from 0 to 127, all different within a row; in each aligned block of 64 rows (0 to 63, 64 to 127, ...) at most 5 rows name the same one
- probs: float32 [8192, 8], P(('expert', 'dp')), may hold values from 0.02 to 1
- cotangent: bfloat16 [8192, 2048], P(('expert', 'dp')), may hold values from -6 to 6
- w_gate: bfloat16 [128, 2048, 384], P('expert'), may hold values from -0.125 to 0.125
- w_up: bfloat16 [128, 2048, 384], P('expert'), may hold values from -0.125 to 0.125
- w_down: bfloat16 [128, 2048, 384], P('expert'), may hold values from -0.3125 to 0.3125
Outputs:
- mixed: bfloat16 [8192, 2048], P(('expert', 'dp'))
- token_grad: bfloat16 [8192, 2048], P(('expert', 'dp'))
- prob_grad: float32 [8192, 8], P(('expert', 'dp'))
- gate_grad: bfloat16 [128, 2048, 384], P('expert', 'dp')
- up_grad: bfloat16 [128, 2048, 384], P('expert', 'dp')
- down_grad: bfloat16 [128, 2048, 384], P('expert', 'dp')
The draws below stay inside these ranges and needn't reach their ends.
Inputs may be any that keep to these rules, and one draw needn't show every extreme that they name: `routes`: each row names 8 different experts. Among the 64 rows of one device no expert is named by more than 5 rows, a bound that some block reaches.
All inputs are finite; a program needn't handle non-finite values.
Results may differ from the reference program's by a relative error of at most 0.0095.
Values may be sent and summed in bfloat16 or wider, within the bound.
A program may use at most 128 MiB of HBM per device.

```python
import math
import jax
import jax.numpy as jnp
import numpy as np
from jax import lax

D = 2048
H = 384
TOP = 8
TOK_DEV = 64
EXPERTS = 128
TOKENS = 8192
CAP = 5
N_EXPERT = 32
N_DP = 4


def level_of(stream_key, dims, cuts, smallest, high):
    gain = 1.0
    for axis_at, shards_of in cuts:
        draws = jax.random.uniform(jax.random.fold_in(jax.random.fold_in(stream_key, 6), axis_at), (shards_of,), jnp.float32, smallest / len(cuts), high / len(cuts))
        gain = gain * jnp.repeat(jnp.exp(draws), dims[axis_at] // shards_of).reshape((-1,) + (1,) * (len(dims) - 1 - axis_at))
    return gain


def deal_out(stream_key, own, number, rows, number_of, top, limit, lean):
    ranking = jax.random.permutation(stream_key, number_of)
    crowded, common = load_shares(number_of, rows * top, limit, lean, True), load_shares(number_of, rows * top, limit, lean, False)
    places = jnp.arange(number_of)

    def named(lengths, rotation):
        used = int((lengths > 0).sum())
        fixed = max(1, used // 4)
        moved = fixed + (places - fixed + rotation * (used - fixed)) % max(1, number_of - fixed)
        return jnp.zeros((number_of,), jnp.int32).at[ranking[jnp.where(places < fixed, places, moved)]].set(jnp.asarray(lengths, jnp.int32))

    lengths = jnp.where(number % 4 == 0, named(crowded, number // 4), named(common, number - number // 4 - 1))
    mixed = jax.random.permutation(jax.random.fold_in(own, 3), number_of)
    source_of, taker = mixed[0:number_of // 2 * 2:2], mixed[1:number_of // 2 * 2:2]
    margin = jnp.minimum(lengths[source_of] - 1, limit - lengths[taker]) // 2
    margin = jnp.where((source_of == ranking[0]) | (taker == ranking[0]) | (lengths[taker] == 0), 0, jnp.maximum(margin, 0))
    moved = jax.random.randint(jax.random.fold_in(own, 4), (number_of // 2,), 0, 1 << 20) % (margin + 1)
    lengths = lengths.at[source_of].add(-moved).at[taker].add(moved)
    labels = jnp.searchsorted(jnp.cumsum(lengths), jnp.arange(rows * top), side="right").astype(jnp.int32)
    listing = labels.reshape(top, rows).T
    listing = listing[jax.random.permutation(jax.random.fold_in(own, 1), rows)]
    rotation = jax.random.randint(jax.random.fold_in(own, 2), (rows, 1), 0, top)
    return jnp.take_along_axis(listing, (jnp.arange(top)[None, :] + rotation) % top, axis=1)


def load_shares(count, total, most, slope, full):
    portions = [(1 << 20) // math.isqrt(standing ** slope) + 1 for standing in range(1, count + 1)]
    largest = most if full else min(most, max(-(-total // count), total * portions[0] // sum(portions)))
    least = 1 if total - largest >= count - 1 else 0
    holding, rest = [largest] + [least] * (count - 1), total - largest - least * (count - 1)
    while rest > 0:
        movable = [i for i in range(1, count) if holding[i] < largest] or [i for i in range(1, count) if holding[i] < most]
        pool, remaining = sum([portions[i] for i in movable]), rest
        for i in movable:
            more = min(most - holding[i], max(1, remaining * portions[i] // pool), rest)
            holding[i] = holding[i] + more
            rest = rest - more
    return np.array(holding)


def normal_values(key, extent, deviation, most, pieces=(), kind=jnp.bfloat16):
    loudness = level_of(key, extent, pieces, -0.22, 0.18) if pieces else 1.0
    values = jax.random.normal(key, extent, jnp.float32) * deviation * loudness
    return jnp.minimum(jnp.maximum(values, -most), most).astype(kind)


def setup_inputs(seed: int = 0) -> dict:
    splits = jax.random.split(jax.random.key(seed), 8)
    tokens = normal_values(splits[0], (TOKENS, D), 1.0, 6.0, ((0, 128),))
    routes_keys = jax.random.split(jax.random.fold_in(splits[1], 1), TOKENS // TOK_DEV)
    routes_turns = jax.random.permutation(jax.random.fold_in(splits[1], 3), TOKENS // TOK_DEV)
    routes = jax.vmap(lambda own, number: deal_out(jax.random.fold_in(splits[1], 2), own, number, TOK_DEV, EXPERTS, TOP, CAP, 2))(routes_keys, routes_turns).reshape((TOKENS, TOP))
    probs = jnp.clip(jnp.exp(math.log(1.0) - 3.912023 * jax.random.uniform(splits[2], (TOKENS, TOP), jnp.float32) ** level_of(splits[2], (TOKENS, TOP), ((0, 128),), -0.2, 0.2)), 0.02, 1.0)
    cotangent = normal_values(splits[3], (TOKENS, D), 1.0, 6.0, ((0, 128),))
    w_gate = normal_values(splits[4], (EXPERTS, D, H), D ** -0.5, 0.125, ((0, 32),))
    w_up = normal_values(splits[5], (EXPERTS, D, H), D ** -0.5, 0.125, ((0, 32),))
    w_down = normal_values(splits[6], (EXPERTS, D, H), H ** -0.5, 0.3125, ((0, 32),))
    return {"tokens": tokens, "routes": routes, "probs": probs, "cotangent": cotangent, "w_gate": w_gate, "w_up": w_up, "w_down": w_down}


def expert_rows(rows_in, upstream, gate_w, up_w, down_w):
    gate_pre = jnp.dot(rows_in, gate_w, preferred_element_type=jnp.float32)
    up_pre = jnp.dot(rows_in, up_w, preferred_element_type=jnp.float32)
    sigmoid_gate = jax.nn.sigmoid(gate_pre)
    active = (gate_pre * sigmoid_gate * up_pre).astype(jnp.bfloat16)
    output = jnp.dot(active, down_w.T, preferred_element_type=jnp.float32).astype(jnp.bfloat16)
    d_active = jnp.dot(upstream, down_w, preferred_element_type=jnp.float32)
    d_gate = (d_active * up_pre * sigmoid_gate * (1.0 + gate_pre * (1.0 - sigmoid_gate))).astype(jnp.bfloat16)
    d_up = (d_active * gate_pre * sigmoid_gate).astype(jnp.bfloat16)
    d_input = (jnp.dot(d_gate, gate_w.T, preferred_element_type=jnp.float32)
               + jnp.dot(d_up, up_w.T, preferred_element_type=jnp.float32)).astype(jnp.bfloat16)
    grad_gate = jnp.dot(rows_in.T, d_gate, preferred_element_type=jnp.float32)
    grad_up = jnp.dot(rows_in.T, d_up, preferred_element_type=jnp.float32)
    grad_down = jnp.dot(upstream.T, active, preferred_element_type=jnp.float32)
    return output, d_input, (grad_gate, grad_up, grad_down)


def round_partial(value):
    return lax.optimization_barrier(value.astype(jnp.bfloat16)).astype(jnp.float32)


def reference(tokens, routes, probs, cotangent, w_gate, w_up, w_down):
    totals = jnp.sum(probs, axis=1, keepdims=True)
    gate_share = probs / totals
    shares_flat = gate_share.reshape(-1)
    flat_expert = routes.reshape(-1).astype(jnp.int32)
    entry_count = TOKENS * TOP
    entry_token = jnp.arange(entry_count, dtype=jnp.int32) // TOP
    replica_of = (entry_token // TOK_DEV) % N_DP
    group_key = (flat_expert * N_DP + replica_of).astype(jnp.int32)
    sort_order = jnp.argsort(group_key, stable=True).astype(jnp.int32)
    group_size = jnp.zeros((EXPERTS * N_DP,), jnp.int32).at[group_key].add(1)
    starts = (jnp.cumsum(group_size) - group_size).astype(jnp.int32)
    row_offset = jnp.arange(N_EXPERT * CAP, dtype=jnp.int32)
    zero_value = jnp.zeros((), jnp.bfloat16)

    def per_expert(state_carry, expert):
        mixed_acc, input_acc, share_acc = state_carry
        gate_w = w_gate[expert]
        up_w = w_up[expert]
        down_w = w_down[expert]
        zero_grad = jnp.zeros((D, H), jnp.float32)
        partials = [zero_grad, zero_grad, zero_grad]
        for replica in range(N_DP):
            group_id = expert * N_DP + replica
            live_row = row_offset < group_size[group_id]
            live_mask = live_row[:, None]
            slot_index = sort_order[jnp.minimum(starts[group_id] + row_offset, entry_count - 1)]
            token_index = slot_index // TOP
            rows_in = jnp.where(live_mask, tokens[token_index], zero_value)
            upstream_row = cotangent[token_index].astype(jnp.float32)
            scaled = (shares_flat[slot_index][:, None] * upstream_row).astype(jnp.bfloat16)
            upstream = jnp.where(live_mask, scaled, zero_value)
            output, d_input, grad_terms = expert_rows(rows_in, upstream, gate_w, up_w, down_w)
            partials = [running + round_partial(addend) for running, addend in zip(partials, grad_terms)]
            out_wide = output.astype(jnp.float32)
            mixed_acc = mixed_acc.at[token_index].add(
                jnp.where(live_mask, shares_flat[slot_index][:, None] * out_wide, 0.0))
            input_acc = input_acc.at[token_index].add(jnp.where(live_mask, d_input.astype(jnp.float32), 0.0))
            share_acc = share_acc.at[slot_index].add(
                jnp.where(live_row, jnp.sum(out_wide * upstream_row, axis=1), 0.0))
        result = tuple(running.astype(jnp.bfloat16) for running in partials)
        return (mixed_acc, input_acc, share_acc), result

    start_state = (jnp.zeros((TOKENS, D), jnp.float32), jnp.zeros((TOKENS, D), jnp.float32),
                   jnp.zeros((entry_count,), jnp.float32))
    final_state, stacked = lax.scan(per_expert, start_state, jnp.arange(EXPERTS, dtype=jnp.int32))
    mixed_acc, input_acc, share_acc = final_state
    share_grad = share_acc.reshape(TOKENS, TOP)
    prob_grad = (share_grad - jnp.sum(gate_share * share_grad, axis=1, keepdims=True)) / totals
    return (mixed_acc.astype(jnp.bfloat16), input_acc.astype(jnp.bfloat16), prob_grad,
            stacked[0], stacked[1], stacked[2])
```

```python
import functools

import jax
import jax.numpy as jnp
import numpy as np
from jax import lax
from jax.experimental import pallas as pl
from jax.experimental.pallas import tpu as pltpu
from jax.sharding import PartitionSpec as P

MESH = pl.DeviceIdType.MESH
CAP = 5
BF = jnp.bfloat16
F32 = jnp.float32
NT = (((1,), (1,)), ((), ()))
TN = (((0,), (0,)), ((), ()))


def mm(a, b, dims=None, precision=None):
    dims = (((1,), (0,)), ((), ())) if dims is None else dims
    return lax.dot_general(a, b, dims, preferred_element_type=F32, precision=precision)


def layer_kernel(
    n_e, n_dp,
    tok_ref, cot_ref, routes_ref, probs_ref, col_ref, row_ref, perm_ref, wg_hbm, wu_hbm, wd_hbm,
    mixed_ref, tgrad_ref, pgrad_ref, gg_hbm, gu_hbm, gd_hbm,
    sa, sb, ra, rb, ro, rd, x, u, q, g, gt, whi, wlo, wg, wu, wd, h, xs, us, pre_g, pre_u,
    w_sem, loc_sem, out_sem, snd, rcv, ysnd_r, yrcv_r, ysnd_h, yrcv_h,
):
    me = lax.axis_index("expert")
    my = lax.axis_index("dp")
    el = wg.shape[0]
    width = tok_ref.shape[1]
    chunk = width // n_dp
    t_n = tok_ref.shape[0]
    top = routes_ref.shape[1]
    n_x = n_e * el
    blocks = n_dp * el
    msg = blocks * CAP
    groups = n_e // blocks
    grows = blocks * msg
    per = blocks * CAP
    gd = 4
    gb = gd * msg

    w_copies = [
        pltpu.make_async_copy(src, dst, w_sem.at[i])
        for i, (src, dst) in enumerate(((wg_hbm, wg), (wu_hbm, wu), (wd_hbm, wd)))
    ]
    for copy in w_copies:
        copy.start()

    barrier = pltpu.get_barrier_semaphore()

    @pl.loop(1, n_e)
    def _(d):
        pl.semaphore_signal(barrier, inc=1, device_id={"expert": lax.rem(me + d, n_e)}, device_id_type=MESH)

    for d in range(1, n_dp):
        pl.semaphore_signal(barrier, inc=1, device_id={"dp": lax.rem(my + d, n_dp)}, device_id_type=MESH)

    routes = routes_ref[...]
    probs = probs_ref[...]
    totals = jnp.sum(probs, axis=1, keepdims=True)
    share = probs / totals
    lane_x = lax.broadcasted_iota(jnp.int32, (t_n, n_x), 1)
    named = jnp.zeros((t_n, n_x), F32)
    share_x = jnp.zeros((t_n, n_x), F32)
    for j in range(top):
        hit = routes[:, j : j + 1] == lane_x
        named = named + jnp.where(hit, 1.0, 0.0)
        share_x = share_x + jnp.where(hit, share[:, j : j + 1], 0.0)
    before = jnp.where(
        lax.broadcasted_iota(jnp.int32, (t_n, t_n), 0) > lax.broadcasted_iota(jnp.int32, (t_n, t_n), 1), 1.0, 0.0
    ).astype(BF)
    rank = mm(before, named.astype(BF))
    place = jnp.where(named > 0.0, rank, -1.0).astype(BF)
    place_c = jnp.concatenate([place] * n_dp, axis=0)
    share_c = jnp.concatenate([share_x] * n_dp, axis=0)
    tok_c = jnp.concatenate([tok_ref[:, c * chunk : (c + 1) * chunk] for c in range(n_dp)], axis=0)
    cot_c = jnp.concatenate([cot_ref[:, c * chunk : (c + 1) * chunk] for c in range(n_dp)], axis=0)

    pl.semaphore_wait(barrier, n_e - 1 + n_dp - 1)

    lane_e = lax.broadcasted_iota(jnp.int32, (gb, n_x), 1)
    lane_c = lax.broadcasted_iota(jnp.int32, (gb, n_dp * t_n), 1) // t_n
    col_e = col_ref[:, 0:1]
    col_s = col_ref[:, 1:2].astype(F32)
    col_c = col_ref[:, 2:3]
    n_g = n_e // gd

    def message(buf, i):
        return buf.at[pl.ds(pl.multiple_of(i * msg, msg), msg)]

    def send(kind, src, dst, o):
        @pl.when(o != me)
        def _():
            pltpu.make_async_remote_copy(
                src_ref=message(src, o), dst_ref=message(dst, me),
                send_sem=snd.at[kind, o], recv_sem=rcv.at[kind, me],
                device_id={"expert": o}, device_id_type=MESH,
            ).start()

        @pl.when(o == me)
        def _():
            pltpu.make_async_copy(message(src, o), message(dst, o), loc_sem.at[kind]).start()

    def await_from(kind, dst, i):
        @pl.when(i != me)
        def _():
            pltpu.make_async_remote_copy(
                src_ref=message(dst, i), dst_ref=message(dst, i),
                send_sem=snd.at[kind, i], recv_sem=rcv.at[kind, i],
                device_id={"expert": i}, device_id_type=MESH,
            ).wait_recv()

        @pl.when(i == me)
        def _():
            pltpu.make_async_copy(message(dst, i), message(dst, i), loc_sem.at[kind]).wait()

    def await_sent(kind, src):
        @pl.loop(0, n_e)
        def _(o):
            @pl.when(o != me)
            def _():
                pltpu.make_async_remote_copy(
                    src_ref=message(src, o), dst_ref=message(src, o),
                    send_sem=snd.at[kind, o], recv_sem=rcv.at[kind, o],
                    device_id={"expert": o}, device_id_type=MESH,
                ).wait_send()

    def await_group(kind, dst, gr):
        @pl.loop(0, blocks)
        def _(i):
            await_from(kind, dst, gr * blocks + i)

    def pick(og):
        return jnp.where(lane_e == col_e + og * (gd * el), 1.0, 0.0)

    @pl.loop(0, n_g)
    def _(i):
        og = lax.rem(me // gd + i, n_g)
        rows = pl.ds(pl.multiple_of(og * gb, gb), gb)
        held = mm(pick(og).astype(BF), place_c, NT)
        chosen = jnp.where((held == col_s) & (lane_c == col_c), 1.0, 0.0).astype(BF)
        g[rows, :] = chosen
        sa[rows, :] = mm(chosen, tok_c).astype(BF)
        for k in range(gd):
            send(0, sa, ra, og * gd + k)

    @pl.loop(0, n_g)
    def _(i):
        og = lax.rem(me // gd + i, n_g)
        rows = pl.ds(pl.multiple_of(og * gb, gb), gb)
        chosen = g[rows, :]
        scale = mm(pick(og), share_c, NT, lax.Precision.HIGHEST)
        scale = jnp.sum(scale * chosen.astype(F32), axis=1, keepdims=True)
        sb[rows, :] = (mm(chosen, cot_c) * scale).astype(BF)
        for k in range(gd):
            send(1, sb, rb, og * gd + k)

    half = grows // 2
    for p in range(2):
        q[p * half : (p + 1) * half, :] = jnp.where(
            lax.broadcasted_iota(jnp.int32, (half, grows), 1) == perm_ref[p * half : (p + 1) * half, 0:1], 1.0, 0.0
        ).astype(BF)
    tcols = n_e * msg // 4
    sub_e = lax.broadcasted_iota(jnp.int32, (n_x, tcols), 0)
    sub_c = lax.broadcasted_iota(jnp.int32, (n_dp * t_n, tcols), 0) // t_n
    for p in range(4):
        cols = slice(p * tcols, (p + 1) * tcols)
        pick_t = jnp.where(sub_e == row_ref[0:1, cols], 1.0, 0.0)
        held = mm(place_c, pick_t.astype(BF))
        here = (held == row_ref[1:2, cols].astype(F32)) & (sub_c == row_ref[2:3, cols])
        gt[:, cols] = jnp.where(here, 1.0, 0.0).astype(BF)
        weight = jnp.where(here, mm(share_c, pick_t, None, lax.Precision.HIGHEST), 0.0)
        high = weight.astype(BF)
        whi[:, cols] = high
        wlo[:, cols] = (weight - high.astype(F32)).astype(BF)

    def regroup(dst_write, src, gr):
        for p in range(2):
            dst_write(p, mm(q[p * half : (p + 1) * half, :], src[gr * grows : (gr + 1) * grows, :]).astype(BF))

    ex_rows = el * per

    def y_rows(kind, src, dst, gr):
        for d in range(1, n_dp):
            to = lax.rem(my + d, n_dp)
            pltpu.make_async_remote_copy(
                src_ref=src.at[gr, to], dst_ref=dst.at[my, gr],
                send_sem=ysnd_r.at[kind, gr, d], recv_sem=yrcv_r.at[kind, gr, my],
                device_id={"dp": to}, device_id_type=MESH,
            ).start()
        pltpu.make_async_copy(src.at[gr, my], dst.at[my, gr], yrcv_r.at[kind, gr, my]).start()

    def y_rows_wait(kind, src, dst, gr):
        for d in range(1, n_dp):
            frm = lax.rem(my + d, n_dp)
            pltpu.make_async_remote_copy(
                src_ref=src.at[gr, frm], dst_ref=dst.at[frm, gr],
                send_sem=ysnd_r.at[kind, gr, d], recv_sem=yrcv_r.at[kind, gr, frm],
                device_id={"dp": frm}, device_id_type=MESH,
            ).wait_recv()
        pltpu.make_async_copy(src.at[gr, my], dst.at[my, gr], yrcv_r.at[kind, gr, my]).wait()

    def y_hidden(kind, wait):
        for d in range(1, n_dp):
            to = lax.rem(my + d, n_dp)
            if wait:
                pltpu.make_async_remote_copy(
                    src_ref=h.at[kind, to], dst_ref=h.at[kind, to],
                    send_sem=ysnd_h.at[kind, d], recv_sem=yrcv_h.at[kind, to],
                    device_id={"dp": to}, device_id_type=MESH,
                ).wait_recv()
            else:
                pltpu.make_async_remote_copy(
                    src_ref=h.at[kind, my], dst_ref=h.at[kind, my],
                    send_sem=ysnd_h.at[kind, d], recv_sem=yrcv_h.at[kind, my],
                    device_id={"dp": to}, device_id_type=MESH,
                ).start()

    def into(dst, gr):
        def write(p, value):
            for c in range(n_dp // 2):
                dst[gr, p * (n_dp // 2) + c] = value[c * ex_rows : (c + 1) * ex_rows]
        return write

    for gr in range(groups):
        await_group(0, ra, gr)
        regroup(into(x, gr), ra, gr)
        y_rows(0, x, xs, gr)

    def rows_of(src, c, e):
        return jnp.concatenate([src[gr, c, pl.ds(pl.multiple_of(e * per, per), per), :] for gr in range(groups)], axis=0)

    def keep_hidden(kind, e, value):
        for gr in range(groups):
            h[kind, my, gr, pl.ds(pl.multiple_of(e * per, per), per), :] = value[gr * per : (gr + 1) * per]

    def keep_rows(dst, c, e, value):
        for gr in range(groups):
            dst[pl.ds(pl.multiple_of(gr * grows + (c * el + e) * per, per), per), :] = value[gr * per : (gr + 1) * per]

    w_copies[0].wait()
    w_copies[1].wait()
    w_copies[2].wait()

    @pl.loop(0, el)
    def _(e):
        gate = 0.0
        up = 0.0
        for c in range(n_dp):
            rows = rows_of(x, c, e)
            gate = gate + mm(rows, wg[e, c * chunk : (c + 1) * chunk, :])
            up = up + mm(rows, wu[e, c * chunk : (c + 1) * chunk, :])
        pre_g[e] = gate
        pre_u[e] = up
        active = (gate * jax.nn.sigmoid(gate) * up).astype(BF)
        keep_hidden(0, e, active)
        for c in range(n_dp):
            keep_rows(ra, c, e, mm(active, wd[e, c * chunk : (c + 1) * chunk, :], NT).astype(BF))

    y_hidden(0, False)
    await_sent(0, sa)

    def plain(dst, gr):
        def write(p, value):
            dst[gr * grows + p * half : gr * grows + (p + 1) * half, :] = value
        return write

    def send_group(kind, src, dst, gr):
        @pl.loop(0, blocks)
        def _(i):
            send(kind, src, dst, gr * blocks + lax.rem(me + i, blocks))

    for gr in range(groups):
        regroup(plain(sa, gr), ra, gr)
        send_group(2, sa, ro, gr)

    for gr in range(groups):
        await_group(1, rb, gr)
        regroup(into(u, gr), rb, gr)
        y_rows(1, u, us, gr)

    @pl.loop(0, el)
    def _(e):
        d_active = 0.0
        for c in range(n_dp):
            d_active = d_active + mm(rows_of(u, c, e), wd[e, c * chunk : (c + 1) * chunk, :])
        gate = pre_g[e]
        up = pre_u[e]
        sig = jax.nn.sigmoid(gate)
        d_gate = (d_active * up * sig * (1.0 + gate * (1.0 - sig))).astype(BF)
        d_up = (d_active * gate * sig).astype(BF)
        keep_hidden(1, e, d_gate)
        keep_hidden(2, e, d_up)
        for c in range(n_dp):
            cols = slice(c * chunk, (c + 1) * chunk)
            keep_rows(rb, c, e, (mm(d_gate, wg[e, cols, :], NT) + mm(d_up, wu[e, cols, :], NT)).astype(BF))

    y_hidden(1, False)
    y_hidden(2, False)
    await_sent(1, sb)
    for gr in range(groups):
        regroup(plain(sb, gr), rb, gr)
        send_group(3, sb, rd, gr)

    for gr in range(groups):
        await_group(2, ro, gr)
    mixed = mm(whi[...], ro[...]) + mm(wlo[...], ro[...])
    for c in range(n_dp):
        mixed_ref[:, c * chunk : (c + 1) * chunk] = mixed[c * t_n : (c + 1) * t_n].astype(BF)
    grad_x = jnp.zeros((n_dp * t_n, n_x), F32)
    for og in range(n_g):
        rows = slice(og * gb, (og + 1) * gb)
        dots = jnp.sum(mm(g[rows, :], cot_c) * ro[rows, :].astype(F32), axis=1, keepdims=True)
        spread = pick(og) * dots
        high = spread.astype(BF)
        low = (spread - high.astype(F32)).astype(BF)
        grad_x = grad_x + mm(gt[:, rows], high) + mm(gt[:, rows], low)
    share_grad_x = grad_x[0:t_n]
    for c in range(1, n_dp):
        share_grad_x = share_grad_x + grad_x[c * t_n : (c + 1) * t_n]
    inner = jnp.sum(share_grad_x * share_x, axis=1, keepdims=True)
    for j in range(top):
        mine = jnp.sum(jnp.where(routes[:, j : j + 1] == lane_x, share_grad_x, 0.0), axis=1, keepdims=True)
        pgrad_ref[:, j : j + 1] = (mine - inner) / totals

    def gathered(src, e):
        return jnp.concatenate(
            [src[r, gr, pl.ds(pl.multiple_of(e * per, per), per), :] for r in range(n_dp) for gr in range(groups)], axis=0
        )

    def hidden_of(kind, e):
        return jnp.concatenate(
            [h[kind, r, gr, pl.ds(pl.multiple_of(e * per, per), per), :] for r in range(n_dp) for gr in range(groups)],
            axis=0,
        )

    y_hidden(0, True)
    for gr in range(groups):
        y_rows_wait(1, u, us, gr)

    @pl.loop(0, el)
    def _(e):
        wg[e, 2 * chunk : 3 * chunk, :] = mm(gathered(us, e), hidden_of(0, e), TN).astype(BF)

    out_d = pltpu.make_async_copy(wg.at[:, 2 * chunk : 3 * chunk], gd_hbm, out_sem.at[2])
    out_d.start()

    for gr in range(groups):
        y_rows_wait(0, x, xs, gr)
    y_hidden(1, True)

    @pl.loop(0, el)
    def _(e):
        wg[e, 0 * chunk : 1 * chunk, :] = mm(gathered(xs, e), hidden_of(1, e), TN).astype(BF)

    out_g = pltpu.make_async_copy(wg.at[:, 0 * chunk : 1 * chunk], gg_hbm, out_sem.at[0])
    out_g.start()
    y_hidden(2, True)

    @pl.loop(0, el)
    def _(e):
        wg[e, 1 * chunk : 2 * chunk, :] = mm(gathered(xs, e), hidden_of(2, e), TN).astype(BF)

    out_u = pltpu.make_async_copy(wg.at[:, 1 * chunk : 2 * chunk], gu_hbm, out_sem.at[1])
    out_u.start()

    for gr in range(groups):
        await_group(3, rd, gr)
    tgrad = mm(gt[...], rd[...])
    for c in range(n_dp):
        tgrad_ref[:, c * chunk : (c + 1) * chunk] = tgrad[c * t_n : (c + 1) * t_n].astype(BF)

    await_sent(2, sa)
    await_sent(3, sb)
    for d in range(1, n_dp):
        to = lax.rem(my + d, n_dp)
        for kind, (src, dst) in enumerate(((x, xs), (u, us))):
            for gr in range(groups):
                pltpu.make_async_remote_copy(
                    src_ref=src.at[gr, to], dst_ref=dst.at[my, gr],
                    send_sem=ysnd_r.at[kind, gr, d], recv_sem=yrcv_r.at[kind, gr, my],
                    device_id={"dp": to}, device_id_type=MESH,
                ).wait_send()
        for kind in range(3):
            pltpu.make_async_remote_copy(
                src_ref=h.at[kind, my], dst_ref=h.at[kind, my],
                send_sem=ysnd_h.at[kind, d], recv_sem=yrcv_h.at[kind, my],
                device_id={"dp": to}, device_id_type=MESH,
            ).wait_send()
    out_d.wait()
    out_g.wait()
    out_u.wait()


def shards(n_e, n_dp, tokens, routes, probs, cotangent, w_gate, w_up, w_down):
    t_n, width = tokens.shape
    el, _, hid = w_gate.shape
    chunk = width // n_dp
    blocks = n_dp * el
    msg = blocks * CAP
    groups = n_e // blocks
    grows = blocks * msg
    slots = n_e * msg
    gb = 4 * msg
    i = np.arange(slots)
    m = i % msg
    local, seat, part = (m % (el * CAP)) // CAP, i % CAP, m // (el * CAP)
    col = np.zeros((gb, 4), np.int32)
    col[:, 0] = ((i // msg) * el + local)[:gb]
    col[:, 1], col[:, 2] = seat[:gb], part[:gb]
    row = np.zeros((8, slots), np.int32)
    row[0], row[1], row[2] = (i // msg) * el + local, seat, part
    j = np.arange(grows)
    perm = (((j % msg) // CAP) * msg + (j // msg) * CAP + j % CAP).astype(np.int32)[:, None]
    vmem = pl.BlockSpec(memory_space=pltpu.VMEM)
    hbm = pl.BlockSpec(memory_space=pl.ANY)
    dma = pltpu.SemaphoreType.DMA
    grad = jax.ShapeDtypeStruct((el, chunk, hid), BF)
    V = pltpu.VMEM
    return pl.pallas_call(
        functools.partial(layer_kernel, n_e, n_dp),
        out_shape=(
            jax.ShapeDtypeStruct((t_n, width), BF),
            jax.ShapeDtypeStruct((t_n, width), BF),
            jax.ShapeDtypeStruct(probs.shape, F32),
            grad, grad, grad,
        ),
        in_specs=[vmem] * 7 + [hbm] * 3,
        out_specs=[vmem] * 3 + [hbm] * 3,
        scratch_shapes=[V((slots, chunk), BF)] * 6
        + [V((groups, n_dp, el * msg, chunk), BF)] * 2
        + [V((grows, grows), BF), V((slots, n_dp * t_n), BF)]
        + [V((n_dp * t_n, slots), BF)] * 3
        + [V(w_gate.shape, BF)] * 3
        + [V((3, n_dp, groups, el * msg, hid), BF)]
        + [V((n_dp, groups, el * msg, chunk), BF)] * 2
        + [V((el, groups * msg, hid), F32)] * 2
        + [dma((3,)), dma((4,)), dma((3,)), dma((4, n_e)), dma((4, n_e)),
           dma((2, groups, n_dp)), dma((2, groups, n_dp)), dma((3, n_dp)), dma((3, n_dp))],
        compiler_params=pltpu.CompilerParams(collective_id=0, has_side_effects=True, vmem_limit_bytes=67043328),
    )(tokens, cotangent, routes, probs, jnp.asarray(col), jnp.asarray(row), jnp.asarray(perm), w_gate, w_up, w_down)


def solution(mesh):
    both = P(("expert", "dp"), None)
    return jax.shard_map(
        functools.partial(shards, mesh.shape["expert"], mesh.shape["dp"]),
        mesh=mesh,
        in_specs=(both, both, both, both) + (P("expert", None, None),) * 3,
        out_specs=(both, both, both) + (P("expert", "dp", None),) * 3,
        check_vma=False,
    )
```

```python
import functools

import jax
import jax.numpy as jnp
import numpy as np
from jax import lax
from jax.experimental import pallas as pl
from jax.experimental.pallas import tpu as pltpu
from jax.sharding import PartitionSpec as P

MESH = pl.DeviceIdType.MESH
CAP = 5
BF = jnp.bfloat16
F32 = jnp.float32
NT = (((1,), (1,)), ((), ()))
TN = (((0,), (0,)), ((), ()))


def mm(a, b, dims=None, precision=None):
    dims = (((1,), (0,)), ((), ())) if dims is None else dims
    return lax.dot_general(a, b, dims, preferred_element_type=F32, precision=precision)


def layer_kernel(
    n_e, n_dp,
    tok_ref, cot_ref, routes_ref, probs_ref, col_ref, row_ref, perm_ref, wg_hbm, wu_hbm, wd_hbm,
    mixed_ref, tgrad_ref, pgrad_ref, gg_hbm, gu_hbm, gd_hbm,
    sa, sb, ra, rb, ro, rd, x, u, q, g, gt, whi, wlo, wg, wu, wd, h, xs, us, pre_g, pre_u,
    w_sem, loc_sem, out_sem, snd, rcv, ysnd_r, yrcv_r, ysnd_h, yrcv_h, ysnd_f, yrcv_f,
):
    me = lax.axis_index("expert")
    my = lax.axis_index("dp")
    el = wg.shape[0]
    width = tok_ref.shape[1]
    chunk = width // n_dp
    t_n = tok_ref.shape[0]
    top = routes_ref.shape[0]
    n_x = n_e * el
    blocks = n_dp * el
    msg = blocks * CAP
    groups = n_e // blocks
    grows = blocks * msg
    per = blocks * CAP
    gd = 4
    gb = gd * msg

    w_copies = [
        pltpu.make_async_copy(src, dst, w_sem.at[i])
        for i, (src, dst) in enumerate(((wg_hbm, wg), (wu_hbm, wu), (wd_hbm, wd)))
    ]
    for copy in w_copies:
        copy.start()

    barrier = pltpu.get_barrier_semaphore()

    @pl.loop(1, n_e)
    def _(d):
        pl.semaphore_signal(barrier, inc=1, device_id={"expert": lax.rem(me + d, n_e)}, device_id_type=MESH)

    for d in range(1, n_dp):
        pl.semaphore_signal(barrier, inc=1, device_id={"dp": lax.rem(my + d, n_dp)}, device_id_type=MESH)

    def eye(n):
        return jnp.where(
            lax.broadcasted_iota(jnp.int32, (n, n), 0) == lax.broadcasted_iota(jnp.int32, (n, n), 1), 1.0, 0.0
        )

    exact = lax.Precision.HIGHEST
    routes = mm(routes_ref[...].astype(F32), eye(top), TN, exact)
    probs = mm(probs_ref[...], eye(top), TN, exact)
    totals = jnp.sum(probs, axis=1, keepdims=True)
    share = probs / totals
    lane_x = lax.broadcasted_iota(jnp.int32, (t_n, n_x), 1)
    lane_f = lane_x.astype(F32)
    named = jnp.zeros((t_n, n_x), F32)
    share_x = jnp.zeros((t_n, n_x), F32)
    for j in range(top):
        hit = routes[:, j : j + 1] == lane_f
        named = named + jnp.where(hit, 1.0, 0.0)
        share_x = share_x + jnp.where(hit, share[:, j : j + 1], 0.0)
    before = jnp.where(
        lax.broadcasted_iota(jnp.int32, (t_n, t_n), 0) > lax.broadcasted_iota(jnp.int32, (t_n, t_n), 1), 1.0, 0.0
    ).astype(BF)
    rank = mm(before, named.astype(BF))
    place = jnp.where(named > 0.0, rank, -1.0).astype(BF)
    place_c = jnp.concatenate([place] * n_dp, axis=0)
    share_c = jnp.concatenate([share_x] * n_dp, axis=0)
    tok_c = jnp.concatenate([tok_ref[:, c * chunk : (c + 1) * chunk] for c in range(n_dp)], axis=0)
    cot_c = jnp.concatenate([cot_ref[:, c * chunk : (c + 1) * chunk] for c in range(n_dp)], axis=0)

    pl.semaphore_wait(barrier, n_e - 1 + n_dp - 1)

    lane_e = lax.broadcasted_iota(jnp.int32, (gb, n_x), 1)
    lane_c = lax.broadcasted_iota(jnp.int32, (gb, n_dp * t_n), 1) // t_n
    col_e = col_ref[:, 0:1]
    col_s = col_ref[:, 1:2].astype(F32)
    col_c = col_ref[:, 2:3]
    n_g = n_e // gd

    halves = 2
    hw = chunk // halves

    def message(buf, i, hf=None):
        rows = pl.ds(pl.multiple_of(i * msg, msg), msg)
        return buf.at[rows] if hf is None else buf.at[rows, pl.ds(hf * hw, hw)]

    def send(kind, src, dst, o, hf):
        @pl.when(o != me)
        def _():
            pltpu.make_async_remote_copy(
                src_ref=message(src, o, hf), dst_ref=message(dst, me, hf),
                send_sem=snd.at[kind, hf, o], recv_sem=rcv.at[kind, hf, me],
                device_id={"expert": o}, device_id_type=MESH,
            ).start()

        @pl.when(o == me)
        def _():
            pltpu.make_async_copy(message(src, o, hf), message(dst, o, hf), loc_sem.at[kind, hf]).start()

    def send_all(kind, src, dst, hf):
        @pl.loop(0, 8)
        def _(i):
            k = i // 2
            z = lax.rem(me // 8 + 2 + 3 * k + 3 * (k // 2) + 2 * (k // 3), 4)
            core = lax.rem(me + i, 2)
            for dx in (2, 1, 3, 0):
                send(kind, src, dst, z * 8 + lax.rem(me // 2 + dx, 4) * 2 + core, hf)

    def await_from(kind, dst, i, hf):
        @pl.when(i != me)
        def _():
            pltpu.make_async_remote_copy(
                src_ref=message(dst, i, hf), dst_ref=message(dst, i, hf),
                send_sem=snd.at[kind, hf, i], recv_sem=rcv.at[kind, hf, i],
                device_id={"expert": i}, device_id_type=MESH,
            ).wait_recv()

        @pl.when(i == me)
        def _():
            pltpu.make_async_copy(message(dst, i, hf), message(dst, i, hf), loc_sem.at[kind, hf]).wait()

    def await_sent(kind, src):
        @pl.loop(0, n_e)
        def _(o):
            @pl.when(o != me)
            def _():
                for hf in range(halves):
                    pltpu.make_async_remote_copy(
                        src_ref=message(src, o, hf), dst_ref=message(src, o, hf),
                        send_sem=snd.at[kind, hf, o], recv_sem=rcv.at[kind, hf, o],
                        device_id={"expert": o}, device_id_type=MESH,
                    ).wait_send()

    def await_all(kind, dst, hf):
        @pl.loop(0, n_e)
        def _(i):
            await_from(kind, dst, i, hf)

    def pick(og):
        return jnp.where(lane_e == col_e + og * (gd * el), 1.0, 0.0)

    @pl.loop(0, n_g)
    def _(i):
        og = lax.rem(me // gd + 5 * i + 5, n_g)
        rows = pl.ds(pl.multiple_of(og * gb, gb), gb)
        held = mm(pick(og).astype(BF), place_c, NT)
        chosen = jnp.where((held == col_s) & (lane_c == col_c), 1.0, 0.0).astype(BF)
        g[rows, :] = chosen
        sa[rows, :] = mm(chosen, tok_c).astype(BF)
        for k in range(gd):
            send(0, sa, ra, og * gd + k, 0)

    send_all(0, sa, ra, 1)

    @pl.loop(0, n_g)
    def _(i):
        og = lax.rem(me // gd + 5 * i + 5, n_g)
        rows = pl.ds(pl.multiple_of(og * gb, gb), gb)
        chosen = g[rows, :]
        scale = mm(pick(og), share_c, NT, lax.Precision.HIGHEST)
        scale = jnp.sum(scale * chosen.astype(F32), axis=1, keepdims=True)
        sb[rows, :] = (mm(chosen, cot_c) * scale).astype(BF)

    send_all(1, sb, rb, 0)
    send_all(1, sb, rb, 1)

    half = grows // 2
    for p in range(2):
        q[p * half : (p + 1) * half, :] = jnp.where(
            lax.broadcasted_iota(jnp.int32, (half, grows), 1) == perm_ref[p * half : (p + 1) * half, 0:1], 1.0, 0.0
        ).astype(BF)
    tcols = n_e * msg // 4
    sub_e = lax.broadcasted_iota(jnp.int32, (n_x, tcols), 0)
    sub_c = lax.broadcasted_iota(jnp.int32, (n_dp * t_n, tcols), 0) // t_n
    for p in range(4):
        cols = slice(p * tcols, (p + 1) * tcols)
        pick_t = jnp.where(sub_e == row_ref[0:1, cols], 1.0, 0.0)
        held = mm(place_c, pick_t.astype(BF))
        here = (held == row_ref[1:2, cols].astype(F32)) & (sub_c == row_ref[2:3, cols])
        gt[:, cols] = jnp.where(here, 1.0, 0.0).astype(BF)
        weight = jnp.where(here, mm(share_c, pick_t, None, lax.Precision.HIGHEST), 0.0)
        high = weight.astype(BF)
        whi[:, cols] = high
        wlo[:, cols] = (weight - high.astype(F32)).astype(BF)

    def regroup(dst_write, src, gr, hf):
        cols = slice(0, chunk) if hf is None else slice(hf * hw, (hf + 1) * hw)
        for p in range(2):
            dst_write(p, mm(q[p * half : (p + 1) * half, :], src[gr * grows : (gr + 1) * grows, cols]).astype(BF))

    ex_rows = el * per

    def y_rows(kind, src, dst, gr, hf):
        cols = pl.ds(hf * hw, hw)
        for d in (1, n_dp - 1, 2):
            to = lax.rem(my + d, n_dp)
            pltpu.make_async_remote_copy(
                src_ref=src.at[gr, to, :, cols], dst_ref=dst.at[my, gr, :, cols],
                send_sem=ysnd_r.at[kind, gr, hf, d], recv_sem=yrcv_r.at[kind, gr, hf, my],
                device_id={"dp": to}, device_id_type=MESH,
            ).start()
        pltpu.make_async_copy(
            src.at[gr, my, :, cols], dst.at[my, gr, :, cols], yrcv_r.at[kind, gr, hf, my]
        ).start()

    def y_rows_wait(kind, src, dst, gr, hf):
        cols = pl.ds(hf * hw, hw)
        for d in range(1, n_dp):
            frm = lax.rem(my + d, n_dp)
            pltpu.make_async_remote_copy(
                src_ref=src.at[gr, frm, :, cols], dst_ref=dst.at[frm, gr, :, cols],
                send_sem=ysnd_r.at[kind, gr, hf, d], recv_sem=yrcv_r.at[kind, gr, hf, frm],
                device_id={"dp": frm}, device_id_type=MESH,
            ).wait_recv()
        pltpu.make_async_copy(
            src.at[gr, my, :, cols], dst.at[my, gr, :, cols], yrcv_r.at[kind, gr, hf, my]
        ).wait()

    far = lax.rem(my + 2, n_dp)
    sides = (lax.rem(my + 1, n_dp), lax.rem(my + n_dp - 1, n_dp))

    def y_hidden(kind):
        for i in range(2):
            pltpu.make_async_remote_copy(
                src_ref=h.at[kind, my], dst_ref=h.at[kind, my],
                send_sem=ysnd_h.at[kind, i], recv_sem=yrcv_h.at[kind, i],
                device_id={"dp": sides[i]}, device_id_type=MESH,
            ).start()

    def hand_on(kind, i):
        held = sides[1 - i]
        pltpu.make_async_remote_copy(
            src_ref=h.at[kind, held], dst_ref=h.at[kind, held],
            send_sem=ysnd_h.at[kind, i], recv_sem=yrcv_h.at[kind, i],
            device_id={"dp": held}, device_id_type=MESH,
        ).wait_recv()
        pltpu.make_async_remote_copy(
            src_ref=h.at[kind, held, i], dst_ref=h.at[kind, held, i],
            send_sem=ysnd_f.at[kind, i], recv_sem=yrcv_f.at[kind, i],
            device_id={"dp": sides[i]}, device_id_type=MESH,
        ).start()

    def y_hidden_far(kind):
        for i in range(2):
            pltpu.make_async_remote_copy(
                src_ref=h.at[kind, far, i], dst_ref=h.at[kind, far, i],
                send_sem=ysnd_f.at[kind, i], recv_sem=yrcv_f.at[kind, i],
                device_id={"dp": sides[i]}, device_id_type=MESH,
            ).wait_recv()

    def into(dst, gr, hf):
        cols = slice(hf * hw, (hf + 1) * hw)

        def write(p, value):
            for c in range(n_dp // 2):
                dst[gr, p * (n_dp // 2) + c, :, cols] = value[c * ex_rows : (c + 1) * ex_rows]
        return write

    for hf in range(halves):
        await_all(0, ra, hf)
        for gr in range(groups):
            regroup(into(x, gr, hf), ra, gr, hf)
            y_rows(0, x, xs, gr, hf)

    def rows_of(src, c, e):
        return jnp.concatenate([src[gr, c, pl.ds(pl.multiple_of(e * per, per), per), :] for gr in range(groups)], axis=0)

    def keep_hidden(kind, e, value):
        for gr in range(groups):
            h[kind, my, gr, pl.ds(pl.multiple_of(e * per, per), per), :] = value[gr * per : (gr + 1) * per]

    def keep_rows(dst, c, e, value):
        for gr in range(groups):
            dst[pl.ds(pl.multiple_of(gr * grows + (c * el + e) * per, per), per), :] = value[gr * per : (gr + 1) * per]

    w_copies[0].wait()
    w_copies[1].wait()
    w_copies[2].wait()

    @pl.loop(0, el)
    def _(e):
        gate = 0.0
        up = 0.0
        for c in range(n_dp):
            rows = rows_of(x, c, e)
            gate = gate + mm(rows, wg[e, c * chunk : (c + 1) * chunk, :])
            up = up + mm(rows, wu[e, c * chunk : (c + 1) * chunk, :])
        pre_g[e] = gate
        pre_u[e] = up
        active = (gate * jax.nn.sigmoid(gate) * up).astype(BF)
        keep_hidden(0, e, active)
        for c in range(n_dp):
            keep_rows(ra, c, e, mm(active, wd[e, c * chunk : (c + 1) * chunk, :], NT).astype(BF))

    y_hidden(0)
    await_sent(0, sa)

    def plain(dst, gr):
        def write(p, value):
            dst[gr * grows + p * half : gr * grows + (p + 1) * half, :] = value
        return write

    for gr in range(groups):
        regroup(plain(sa, gr), ra, gr, None)
    for hf in range(halves):
        send_all(2, sa, ro, hf)

    for hf in range(halves):
        await_all(1, rb, hf)
        for gr in range(groups):
            regroup(into(u, gr, hf), rb, gr, hf)
        if hf == 0:
            hand_on(0, 0)
            hand_on(0, 1)
        for gr in range(groups):
            y_rows(1, u, us, gr, hf)

    @pl.loop(0, el)
    def _(e):
        d_active = 0.0
        for c in range(n_dp):
            d_active = d_active + mm(rows_of(u, c, e), wd[e, c * chunk : (c + 1) * chunk, :])
        gate = pre_g[e]
        up = pre_u[e]
        sig = jax.nn.sigmoid(gate)
        d_gate = (d_active * up * sig * (1.0 + gate * (1.0 - sig))).astype(BF)
        d_up = (d_active * gate * sig).astype(BF)
        keep_hidden(1, e, d_gate)
        keep_hidden(2, e, d_up)
        for c in range(n_dp):
            cols = slice(c * chunk, (c + 1) * chunk)
            keep_rows(rb, c, e, (mm(d_gate, wg[e, cols, :], NT) + mm(d_up, wu[e, cols, :], NT)).astype(BF))

    y_hidden(1)
    y_hidden(2)
    await_sent(1, sb)
    for gr in range(groups):
        regroup(plain(sb, gr), rb, gr, None)
    for hf in range(halves):
        send_all(3, sb, rd, hf)

    for hf in range(halves):
        await_all(2, ro, hf)
    mixed = mm(whi[...], ro[...]) + mm(wlo[...], ro[...])
    for c in range(n_dp):
        mixed_ref[:, c * chunk : (c + 1) * chunk] = mixed[c * t_n : (c + 1) * t_n].astype(BF)
    grad_x = jnp.zeros((n_dp * t_n, n_x), F32)
    for og in range(n_g):
        rows = slice(og * gb, (og + 1) * gb)
        dots = jnp.sum(mm(g[rows, :], cot_c) * ro[rows, :].astype(F32), axis=1, keepdims=True)
        spread = pick(og) * dots
        high = spread.astype(BF)
        low = (spread - high.astype(F32)).astype(BF)
        grad_x = grad_x + mm(gt[:, rows], high) + mm(gt[:, rows], low)
    share_grad_x = grad_x[0:t_n]
    for c in range(1, n_dp):
        share_grad_x = share_grad_x + grad_x[c * t_n : (c + 1) * t_n]
    inner = jnp.sum(share_grad_x * share_x, axis=1, keepdims=True)
    grads = []
    for j in range(top):
        mine = jnp.sum(jnp.where(routes[:, j : j + 1] == lane_f, share_grad_x, 0.0), axis=1, keepdims=True)
        grads.append((mine - inner) / totals)
    lane_j = lax.broadcasted_iota(jnp.int32, (t_n, top), 1)
    prob_grad = jnp.zeros((t_n, top), F32)
    for j in range(top):
        prob_grad = jnp.where(lane_j == j, grads[j], prob_grad)
    pgrad_ref[...] = mm(prob_grad, eye(t_n), TN, exact)

    def gathered(src, e):
        return jnp.concatenate(
            [src[r, gr, pl.ds(pl.multiple_of(e * per, per), per), :] for r in range(n_dp) for gr in range(groups)], axis=0
        )

    def hidden_of(kind, e):
        return jnp.concatenate(
            [h[kind, r, gr, pl.ds(pl.multiple_of(e * per, per), per), :] for r in range(n_dp) for gr in range(groups)],
            axis=0,
        )

    y_hidden_far(0)
    for hf in range(halves):
        for gr in range(groups):
            y_rows_wait(1, u, us, gr, hf)
            y_rows_wait(0, x, xs, gr, hf)

    @pl.loop(0, el)
    def _(e):
        wg[e, 2 * chunk : 3 * chunk, :] = mm(gathered(us, e), hidden_of(0, e), TN).astype(BF)

    out_d = pltpu.make_async_copy(wg.at[:, 2 * chunk : 3 * chunk], gd_hbm, out_sem.at[2])
    out_d.start()

    for kind in (1, 2):
        hand_on(kind, 0)
        hand_on(kind, 1)

    for hf in range(halves):
        await_all(3, rd, hf)
    tgrad = mm(gt[...], rd[...])
    for c in range(n_dp):
        tgrad_ref[:, c * chunk : (c + 1) * chunk] = tgrad[c * t_n : (c + 1) * t_n].astype(BF)

    y_hidden_far(1)

    @pl.loop(0, el)
    def _(e):
        wg[e, 0 * chunk : 1 * chunk, :] = mm(gathered(xs, e), hidden_of(1, e), TN).astype(BF)

    out_g = pltpu.make_async_copy(wg.at[:, 0 * chunk : 1 * chunk], gg_hbm, out_sem.at[0])
    out_g.start()
    y_hidden_far(2)

    @pl.loop(0, el)
    def _(e):
        wg[e, 1 * chunk : 2 * chunk, :] = mm(gathered(xs, e), hidden_of(2, e), TN).astype(BF)

    out_u = pltpu.make_async_copy(wg.at[:, 1 * chunk : 2 * chunk], gu_hbm, out_sem.at[1])
    out_u.start()

    await_sent(2, sa)
    await_sent(3, sb)
    for d in range(1, n_dp):
        to = lax.rem(my + d, n_dp)
        for kind, (src, dst) in enumerate(((x, xs), (u, us))):
            for gr in range(groups):
                for hf in range(halves):
                    cols = pl.ds(hf * hw, hw)
                    pltpu.make_async_remote_copy(
                        src_ref=src.at[gr, to, :, cols], dst_ref=dst.at[my, gr, :, cols],
                        send_sem=ysnd_r.at[kind, gr, hf, d], recv_sem=yrcv_r.at[kind, gr, hf, my],
                        device_id={"dp": to}, device_id_type=MESH,
                    ).wait_send()
    for kind in range(3):
        for i in range(2):
            pltpu.make_async_remote_copy(
                src_ref=h.at[kind, my], dst_ref=h.at[kind, my],
                send_sem=ysnd_h.at[kind, i], recv_sem=yrcv_h.at[kind, i],
                device_id={"dp": sides[i]}, device_id_type=MESH,
            ).wait_send()
            pltpu.make_async_remote_copy(
                src_ref=h.at[kind, my, i], dst_ref=h.at[kind, my, i],
                send_sem=ysnd_f.at[kind, i], recv_sem=yrcv_f.at[kind, i],
                device_id={"dp": sides[i]}, device_id_type=MESH,
            ).wait_send()
    out_d.wait()
    out_g.wait()
    out_u.wait()


def hand_out(*refs):
    count = (len(refs) - 1) // 3
    srcs, dsts, held, sem = refs[:count], refs[count : 2 * count], refs[2 * count : 3 * count], refs[-1]
    inward = [pltpu.make_async_copy(srcs[i], held[i], sem.at[0, i]) for i in range(count)]
    outward = [pltpu.make_async_copy(held[i], dsts[i], sem.at[1, i]) for i in range(count)]
    for copy in inward:
        copy.start()
    for i in range(count):
        inward[i].wait()
        outward[i].start()
    for copy in outward:
        copy.wait()


def shards(n_e, n_dp, tokens, routes, probs, cotangent, w_gate, w_up, w_down):
    t_n, width = tokens.shape
    el, _, hid = w_gate.shape
    chunk = width // n_dp
    blocks = n_dp * el
    msg = blocks * CAP
    groups = n_e // blocks
    grows = blocks * msg
    slots = n_e * msg
    gb = 4 * msg
    i = np.arange(slots)
    m = i % msg
    local, seat, part = (m % (el * CAP)) // CAP, i % CAP, m // (el * CAP)
    col = np.zeros((gb, 4), np.int32)
    col[:, 0] = ((i // msg) * el + local)[:gb]
    col[:, 1], col[:, 2] = seat[:gb], part[:gb]
    row = np.zeros((8, slots), np.int32)
    row[0], row[1], row[2] = (i // msg) * el + local, seat, part
    j = np.arange(grows)
    perm = (((j % msg) // CAP) * msg + (j // msg) * CAP + j % CAP).astype(np.int32)[:, None]
    vmem = pl.BlockSpec(memory_space=pltpu.VMEM)
    hbm = pl.BlockSpec(memory_space=pl.ANY)
    dma = pltpu.SemaphoreType.DMA
    grad = jax.ShapeDtypeStruct((el, chunk, hid), BF)
    V = pltpu.VMEM
    results = pl.pallas_call(
        functools.partial(layer_kernel, n_e, n_dp),
        out_shape=(
            jax.ShapeDtypeStruct((t_n, width), BF),
            jax.ShapeDtypeStruct((t_n, width), BF),
            jax.ShapeDtypeStruct(probs.shape[::-1], F32),
            grad, grad, grad,
        ),
        in_specs=[vmem] * 7 + [hbm] * 3,
        out_specs=[vmem] * 3 + [hbm] * 3,
        scratch_shapes=[V((slots, chunk), BF)] * 6
        + [V((groups, n_dp, el * msg, chunk), BF)] * 2
        + [V((grows, grows), BF), V((slots, n_dp * t_n), BF)]
        + [V((n_dp * t_n, slots), BF)] * 3
        + [V(w_gate.shape, BF)] * 3
        + [V((3, n_dp, groups, el * msg, hid), BF)]
        + [V((n_dp, groups, el * msg, chunk), BF)] * 2
        + [V((el, groups * msg, hid), F32)] * 2
        + [dma((3,)), dma((4, 2)), dma((3,)), dma((4, 2, n_e)), dma((4, 2, n_e)),
           dma((2, groups, 2, n_dp)), dma((2, groups, 2, n_dp))] + [dma((3, 2))] * 4,
        compiler_params=pltpu.CompilerParams(collective_id=0, has_side_effects=True, vmem_limit_bytes=67043328),
    )(tokens, cotangent, routes.T, probs.T, jnp.asarray(col), jnp.asarray(row), jnp.asarray(perm), w_gate, w_up, w_down)
    shapes = [jax.ShapeDtypeStruct(r.shape, r.dtype) for r in results]
    count = len(shapes)
    mixed, tgrad, pgrad, *grads = pl.pallas_call(
        hand_out,
        out_shape=shapes,
        in_specs=[hbm] * count,
        out_specs=[hbm] * count,
        scratch_shapes=[V(r.shape, r.dtype) for r in shapes] + [dma((2, count))],
    )(*results)
    return mixed, tgrad, pgrad.T, *grads


def solution(mesh):
    both = P(("expert", "dp"), None)
    return jax.shard_map(
        functools.partial(shards, mesh.shape["expert"], mesh.shape["dp"]),
        mesh=mesh,
        in_specs=(both, both, both, both) + (P("expert", None, None),) * 3,
        out_specs=(both, both, both) + (P("expert", "dp", None),) * 3,
        check_vma=False,
    )
```

```python
import functools

import jax
import jax.numpy as jnp
import numpy as np
from jax import lax
from jax.experimental import pallas as pl
from jax.experimental.pallas import tpu as pltpu
from jax.sharding import PartitionSpec as P

MESH = pl.DeviceIdType.MESH
CAP = 5
BF = jnp.bfloat16
F32 = jnp.float32
NT = (((1,), (1,)), ((), ()))
TN = (((0,), (0,)), ((), ()))


def mm(a, b, dims=None, precision=None):
    dims = (((1,), (0,)), ((), ())) if dims is None else dims
    return lax.dot_general(a, b, dims, preferred_element_type=F32, precision=precision)


def layer_kernel(
    n_e, n_dp,
    tok_in, cot_in, routes_in, probs_in, col_in, row_in, perm_in, wg_hbm, wu_hbm, wd_hbm,
    mixed_ref, tgrad_ref, pgrad_ref, gg_hbm, gu_hbm, gd_hbm,
    sa, sb, ra, rb, ro, rd, x, u, q, g, gt, whi, wlo, wg, wu, wd, h, xs, us, pre_g, pre_u,
    tok_ref, cot_ref, routes_ref, probs_ref, col_ref, row_ref, perm_ref,
    in_sem, w_sem, loc_sem, out_sem, snd, rcv, ysnd_r, yrcv_r, ysnd_h, yrcv_h, ysnd_f, yrcv_f,
):
    me = lax.axis_index("expert")
    my = lax.axis_index("dp")
    el = wg.shape[0]
    width = tok_ref.shape[1]
    chunk = width // n_dp
    t_n = tok_ref.shape[0]
    top = routes_ref.shape[0]
    n_x = n_e * el
    blocks = n_dp * el
    msg = blocks * CAP
    groups = n_e // blocks
    grows = blocks * msg
    per = blocks * CAP
    gd = 4
    gb = gd * msg

    barrier = pltpu.get_barrier_semaphore()

    @pl.loop(1, n_e)
    def _(d):
        pl.semaphore_signal(barrier, inc=1, device_id={"expert": lax.rem(me + d, n_e)}, device_id_type=MESH)

    for d in range(1, n_dp):
        pl.semaphore_signal(barrier, inc=1, device_id={"dp": lax.rem(my + d, n_dp)}, device_id_type=MESH)

    in_copies = [
        pltpu.make_async_copy(src, dst, in_sem.at[i])
        for i, (src, dst) in enumerate((
            (routes_in, routes_ref), (probs_in, probs_ref), (col_in, col_ref), (tok_in, tok_ref),
            (cot_in, cot_ref), (row_in, row_ref), (perm_in, perm_ref),
        ))
    ]
    w_copies = [
        pltpu.make_async_copy(src, dst, w_sem.at[i])
        for i, (src, dst) in enumerate(((wg_hbm, wg), (wu_hbm, wu), (wd_hbm, wd)))
    ]
    for copy in in_copies + w_copies:
        copy.start()
    for copy in in_copies[:4]:
        copy.wait()

    def eye(n):
        return jnp.where(
            lax.broadcasted_iota(jnp.int32, (n, n), 0) == lax.broadcasted_iota(jnp.int32, (n, n), 1), 1.0, 0.0
        )

    exact = lax.Precision.HIGHEST
    routes = mm(routes_ref[...].astype(F32), eye(top), TN, exact)
    probs = mm(probs_ref[...], eye(top), TN, exact)
    totals = jnp.sum(probs, axis=1, keepdims=True)
    share = probs / totals
    lane_x = lax.broadcasted_iota(jnp.int32, (t_n, n_x), 1)
    lane_f = lane_x.astype(F32)
    named = jnp.zeros((t_n, n_x), F32)
    share_x = jnp.zeros((t_n, n_x), F32)
    for j in range(top):
        hit = routes[:, j : j + 1] == lane_f
        named = named + jnp.where(hit, 1.0, 0.0)
        share_x = share_x + jnp.where(hit, share[:, j : j + 1], 0.0)
    before = jnp.where(
        lax.broadcasted_iota(jnp.int32, (t_n, t_n), 0) > lax.broadcasted_iota(jnp.int32, (t_n, t_n), 1), 1.0, 0.0
    ).astype(BF)
    rank = mm(before, named.astype(BF))
    place = jnp.where(named > 0.0, rank, -1.0).astype(BF)
    place_c = jnp.concatenate([place] * n_dp, axis=0)
    share_c = jnp.concatenate([share_x] * n_dp, axis=0)
    tok_c = jnp.concatenate([tok_ref[:, c * chunk : (c + 1) * chunk] for c in range(n_dp)], axis=0)

    lane_e = lax.broadcasted_iota(jnp.int32, (gb, n_x), 1)
    lane_c = lax.broadcasted_iota(jnp.int32, (gb, n_dp * t_n), 1) // t_n
    col_e = col_ref[:, 0:1]
    col_s = col_ref[:, 1:2].astype(F32)
    col_c = col_ref[:, 2:3]
    n_g = n_e // gd

    pieces = (4, 2, 2, 2)

    def span(kind, hf):
        wide = chunk // pieces[kind]
        return pl.ds(hf * wide, wide)

    def message(kind, buf, i, hf):
        return buf.at[pl.ds(pl.multiple_of(i * msg, msg), msg), span(kind, hf)]

    def send(kind, src, dst, o, hf):
        @pl.when(o != me)
        def _():
            pltpu.make_async_remote_copy(
                src_ref=message(kind, src, o, hf), dst_ref=message(kind, dst, me, hf),
                send_sem=snd.at[kind, hf, o], recv_sem=rcv.at[kind, hf, me],
                device_id={"expert": o}, device_id_type=MESH,
            ).start()

        @pl.when(o == me)
        def _():
            pltpu.make_async_copy(message(kind, src, o, hf), message(kind, dst, o, hf), loc_sem.at[kind, hf]).start()

    def send_all(kind, src, dst, hf):
        @pl.loop(0, 8)
        def _(i):
            k = i // 2
            z = lax.rem(me // 8 + 2 + 3 * k + 3 * (k // 2) + 2 * (k // 3), 4)
            core = lax.rem(me + i, 2)
            for dx in (2, 1, 3, 0):
                send(kind, src, dst, z * 8 + lax.rem(me // 2 + dx, 4) * 2 + core, hf)

    def await_from(kind, dst, i, hf):
        @pl.when(i != me)
        def _():
            pltpu.make_async_remote_copy(
                src_ref=message(kind, dst, i, hf), dst_ref=message(kind, dst, i, hf),
                send_sem=snd.at[kind, hf, i], recv_sem=rcv.at[kind, hf, i],
                device_id={"expert": i}, device_id_type=MESH,
            ).wait_recv()

        @pl.when(i == me)
        def _():
            pltpu.make_async_copy(message(kind, dst, i, hf), message(kind, dst, i, hf), loc_sem.at[kind, hf]).wait()

    def await_sent(kind, src):
        @pl.loop(0, n_e)
        def _(o):
            @pl.when(o != me)
            def _():
                for hf in range(pieces[kind]):
                    pltpu.make_async_remote_copy(
                        src_ref=message(kind, src, o, hf), dst_ref=message(kind, src, o, hf),
                        send_sem=snd.at[kind, hf, o], recv_sem=rcv.at[kind, hf, o],
                        device_id={"expert": o}, device_id_type=MESH,
                    ).wait_send()

    def await_all(kind, dst, hf):
        @pl.loop(0, n_e)
        def _(i):
            await_from(kind, dst, i, hf)

    def pick(og):
        return jnp.where(lane_e == col_e + og * (gd * el), 1.0, 0.0)

    @pl.loop(0, n_g)
    def _(i):
        og = lax.rem(me // gd + 5 * i + 5, n_g)
        rows = pl.ds(pl.multiple_of(og * gb, gb), gb)
        held = mm(pick(og).astype(BF), place_c, NT)
        chosen = jnp.where((held == col_s) & (lane_c == col_c), 1.0, 0.0).astype(BF)
        g[rows, :] = chosen
        sa[rows, :] = mm(chosen, tok_c).astype(BF)

    pl.semaphore_wait(barrier, n_e - 1 + n_dp - 1)
    for hf in range(pieces[0]):
        send_all(0, sa, ra, hf)

    for copy in in_copies[4:]:
        copy.wait()
    cot_c = jnp.concatenate([cot_ref[:, c * chunk : (c + 1) * chunk] for c in range(n_dp)], axis=0)

    @pl.loop(0, n_g)
    def _(i):
        og = lax.rem(me // gd + 5 * i + 5, n_g)
        rows = pl.ds(pl.multiple_of(og * gb, gb), gb)
        chosen = g[rows, :]
        scale = mm(pick(og), share_c, NT, lax.Precision.HIGHEST)
        scale = jnp.sum(scale * chosen.astype(F32), axis=1, keepdims=True)
        sb[rows, :] = (mm(chosen, cot_c) * scale).astype(BF)

    send_all(1, sb, rb, 0)
    send_all(1, sb, rb, 1)

    half = grows // 2
    for p in range(2):
        q[p * half : (p + 1) * half, :] = jnp.where(
            lax.broadcasted_iota(jnp.int32, (half, grows), 1) == perm_ref[p * half : (p + 1) * half, 0:1], 1.0, 0.0
        ).astype(BF)
    tcols = n_e * msg // 4
    sub_e = lax.broadcasted_iota(jnp.int32, (n_x, tcols), 0)
    sub_c = lax.broadcasted_iota(jnp.int32, (n_dp * t_n, tcols), 0) // t_n
    for p in range(4):
        cols = slice(p * tcols, (p + 1) * tcols)
        pick_t = jnp.where(sub_e == row_ref[0:1, cols], 1.0, 0.0)
        held = mm(place_c, pick_t.astype(BF))
        here = (held == row_ref[1:2, cols].astype(F32)) & (sub_c == row_ref[2:3, cols])
        gt[:, cols] = jnp.where(here, 1.0, 0.0).astype(BF)
        weight = jnp.where(here, mm(share_c, pick_t, None, lax.Precision.HIGHEST), 0.0)
        high = weight.astype(BF)
        whi[:, cols] = high
        wlo[:, cols] = (weight - high.astype(F32)).astype(BF)

    def regroup(dst_write, src, gr, cols):
        for p in range(2):
            dst_write(p, mm(q[p * half : (p + 1) * half, :], src[gr * grows : (gr + 1) * grows, cols]).astype(BF))

    ex_rows = el * per

    def y_rows(kind, src, dst, gr, hf):
        cols = span(kind, hf)
        for d in (1, n_dp - 1, 2):
            to = lax.rem(my + d, n_dp)
            pltpu.make_async_remote_copy(
                src_ref=src.at[gr, to, :, cols], dst_ref=dst.at[my, gr, :, cols],
                send_sem=ysnd_r.at[kind, gr, hf, d], recv_sem=yrcv_r.at[kind, gr, hf, my],
                device_id={"dp": to}, device_id_type=MESH,
            ).start()
        pltpu.make_async_copy(
            src.at[gr, my, :, cols], dst.at[my, gr, :, cols], yrcv_r.at[kind, gr, hf, my]
        ).start()

    def y_rows_wait(kind, src, dst, gr, hf):
        cols = span(kind, hf)
        for d in range(1, n_dp):
            frm = lax.rem(my + d, n_dp)
            pltpu.make_async_remote_copy(
                src_ref=src.at[gr, frm, :, cols], dst_ref=dst.at[frm, gr, :, cols],
                send_sem=ysnd_r.at[kind, gr, hf, d], recv_sem=yrcv_r.at[kind, gr, hf, frm],
                device_id={"dp": frm}, device_id_type=MESH,
            ).wait_recv()
        pltpu.make_async_copy(
            src.at[gr, my, :, cols], dst.at[my, gr, :, cols], yrcv_r.at[kind, gr, hf, my]
        ).wait()

    far = lax.rem(my + 2, n_dp)
    sides = (lax.rem(my + 1, n_dp), lax.rem(my + n_dp - 1, n_dp))

    def y_hidden(kind):
        for i in range(2):
            pltpu.make_async_remote_copy(
                src_ref=h.at[kind, my], dst_ref=h.at[kind, my],
                send_sem=ysnd_h.at[kind, i], recv_sem=yrcv_h.at[kind, i],
                device_id={"dp": sides[i]}, device_id_type=MESH,
            ).start()

    def hand_on(kind, i):
        held = sides[1 - i]
        pltpu.make_async_remote_copy(
            src_ref=h.at[kind, held], dst_ref=h.at[kind, held],
            send_sem=ysnd_h.at[kind, i], recv_sem=yrcv_h.at[kind, i],
            device_id={"dp": held}, device_id_type=MESH,
        ).wait_recv()
        pltpu.make_async_remote_copy(
            src_ref=h.at[kind, held, i], dst_ref=h.at[kind, held, i],
            send_sem=ysnd_f.at[kind, i], recv_sem=yrcv_f.at[kind, i],
            device_id={"dp": sides[i]}, device_id_type=MESH,
        ).start()

    def y_hidden_far(kind):
        for i in range(2):
            pltpu.make_async_remote_copy(
                src_ref=h.at[kind, far, i], dst_ref=h.at[kind, far, i],
                send_sem=ysnd_f.at[kind, i], recv_sem=yrcv_f.at[kind, i],
                device_id={"dp": sides[i]}, device_id_type=MESH,
            ).wait_recv()

    def into(dst, gr, cols):
        def write(p, value):
            for c in range(n_dp // 2):
                dst[gr, p * (n_dp // 2) + c, :, cols] = value[c * ex_rows : (c + 1) * ex_rows]
        return write

    for hf in range(pieces[0]):
        await_all(0, ra, hf)
        for gr in range(groups):
            regroup(into(x, gr, span(0, hf)), ra, gr, span(0, hf))
            y_rows(0, x, xs, gr, hf)

    def rows_of(src, c, e):
        return jnp.concatenate([src[gr, c, pl.ds(pl.multiple_of(e * per, per), per), :] for gr in range(groups)], axis=0)

    def keep_hidden(kind, e, value):
        for gr in range(groups):
            h[kind, my, gr, pl.ds(pl.multiple_of(e * per, per), per), :] = value[gr * per : (gr + 1) * per]

    def keep_rows(dst, c, e, value):
        for gr in range(groups):
            dst[pl.ds(pl.multiple_of(gr * grows + (c * el + e) * per, per), per), :] = value[gr * per : (gr + 1) * per]

    w_copies[0].wait()
    w_copies[1].wait()
    w_copies[2].wait()

    @pl.loop(0, el)
    def _(e):
        gate = 0.0
        up = 0.0
        for c in range(n_dp):
            rows = rows_of(x, c, e)
            gate = gate + mm(rows, wg[e, c * chunk : (c + 1) * chunk, :])
            up = up + mm(rows, wu[e, c * chunk : (c + 1) * chunk, :])
        pre_g[e] = gate
        pre_u[e] = up
        active = (gate * jax.nn.sigmoid(gate) * up).astype(BF)
        keep_hidden(0, e, active)
        for c in range(n_dp):
            keep_rows(ra, c, e, mm(active, wd[e, c * chunk : (c + 1) * chunk, :], NT).astype(BF))

    y_hidden(0)
    await_sent(0, sa)

    def plain(dst, gr):
        def write(p, value):
            dst[gr * grows + p * half : gr * grows + (p + 1) * half, :] = value
        return write

    for gr in range(groups):
        regroup(plain(sa, gr), ra, gr, slice(0, chunk))
    for hf in range(pieces[2]):
        send_all(2, sa, ro, hf)

    for hf in range(pieces[1]):
        await_all(1, rb, hf)
        for gr in range(groups):
            regroup(into(u, gr, span(1, hf)), rb, gr, span(1, hf))
        if hf == 0:
            hand_on(0, 0)
            hand_on(0, 1)
        for gr in range(groups):
            y_rows(1, u, us, gr, hf)

    @pl.loop(0, el)
    def _(e):
        d_active = 0.0
        for c in range(n_dp):
            d_active = d_active + mm(rows_of(u, c, e), wd[e, c * chunk : (c + 1) * chunk, :])
        gate = pre_g[e]
        up = pre_u[e]
        sig = jax.nn.sigmoid(gate)
        d_gate = (d_active * up * sig * (1.0 + gate * (1.0 - sig))).astype(BF)
        d_up = (d_active * gate * sig).astype(BF)
        keep_hidden(1, e, d_gate)
        keep_hidden(2, e, d_up)
        for c in range(n_dp):
            cols = slice(c * chunk, (c + 1) * chunk)
            keep_rows(rb, c, e, (mm(d_gate, wg[e, cols, :], NT) + mm(d_up, wu[e, cols, :], NT)).astype(BF))

    y_hidden(1)
    y_hidden(2)
    await_sent(1, sb)
    for gr in range(groups):
        regroup(plain(sb, gr), rb, gr, slice(0, chunk))
    for hf in range(pieces[3]):
        send_all(3, sb, rd, hf)

    for hf in range(pieces[2]):
        await_all(2, ro, hf)
    mixed = mm(whi[...], ro[...]) + mm(wlo[...], ro[...])
    for c in range(n_dp):
        mixed_ref[:, c * chunk : (c + 1) * chunk] = mixed[c * t_n : (c + 1) * t_n].astype(BF)
    grad_x = jnp.zeros((n_dp * t_n, n_x), F32)
    for og in range(n_g):
        rows = slice(og * gb, (og + 1) * gb)
        dots = jnp.sum(mm(g[rows, :], cot_c) * ro[rows, :].astype(F32), axis=1, keepdims=True)
        spread = pick(og) * dots
        high = spread.astype(BF)
        low = (spread - high.astype(F32)).astype(BF)
        grad_x = grad_x + mm(gt[:, rows], high) + mm(gt[:, rows], low)
    share_grad_x = grad_x[0:t_n]
    for c in range(1, n_dp):
        share_grad_x = share_grad_x + grad_x[c * t_n : (c + 1) * t_n]
    inner = jnp.sum(share_grad_x * share_x, axis=1, keepdims=True)
    grads = []
    for j in range(top):
        mine = jnp.sum(jnp.where(routes[:, j : j + 1] == lane_f, share_grad_x, 0.0), axis=1, keepdims=True)
        grads.append((mine - inner) / totals)
    lane_j = lax.broadcasted_iota(jnp.int32, (t_n, top), 1)
    prob_grad = jnp.zeros((t_n, top), F32)
    for j in range(top):
        prob_grad = jnp.where(lane_j == j, grads[j], prob_grad)
    pgrad_ref[...] = mm(prob_grad, eye(t_n), TN, exact)

    def gathered(src, e):
        return jnp.concatenate(
            [src[r, gr, pl.ds(pl.multiple_of(e * per, per), per), :] for r in range(n_dp) for gr in range(groups)], axis=0
        )

    def hidden_of(kind, e):
        return jnp.concatenate(
            [h[kind, r, gr, pl.ds(pl.multiple_of(e * per, per), per), :] for r in range(n_dp) for gr in range(groups)],
            axis=0,
        )

    y_hidden_far(0)
    for kind, (src, dst) in enumerate(((x, xs), (u, us))):
        for hf in range(pieces[kind]):
            for gr in range(groups):
                y_rows_wait(kind, src, dst, gr, hf)

    @pl.loop(0, el)
    def _(e):
        wg[e, 2 * chunk : 3 * chunk, :] = mm(gathered(us, e), hidden_of(0, e), TN).astype(BF)

    out_d = pltpu.make_async_copy(wg.at[:, 2 * chunk : 3 * chunk], gd_hbm, out_sem.at[2])
    out_d.start()

    for kind in (1, 2):
        hand_on(kind, 0)
        hand_on(kind, 1)

    for hf in range(pieces[3]):
        await_all(3, rd, hf)
    tgrad = mm(gt[...], rd[...])
    for c in range(n_dp):
        tgrad_ref[:, c * chunk : (c + 1) * chunk] = tgrad[c * t_n : (c + 1) * t_n].astype(BF)

    y_hidden_far(1)

    @pl.loop(0, el)
    def _(e):
        wg[e, 0 * chunk : 1 * chunk, :] = mm(gathered(xs, e), hidden_of(1, e), TN).astype(BF)

    out_g = pltpu.make_async_copy(wg.at[:, 0 * chunk : 1 * chunk], gg_hbm, out_sem.at[0])
    out_g.start()
    y_hidden_far(2)

    @pl.loop(0, el)
    def _(e):
        wg[e, 1 * chunk : 2 * chunk, :] = mm(gathered(xs, e), hidden_of(2, e), TN).astype(BF)

    out_u = pltpu.make_async_copy(wg.at[:, 1 * chunk : 2 * chunk], gu_hbm, out_sem.at[1])
    out_u.start()

    await_sent(2, sa)
    await_sent(3, sb)
    for d in range(1, n_dp):
        to = lax.rem(my + d, n_dp)
        for kind, (src, dst) in enumerate(((x, xs), (u, us))):
            for gr in range(groups):
                for hf in range(pieces[kind]):
                    cols = span(kind, hf)
                    pltpu.make_async_remote_copy(
                        src_ref=src.at[gr, to, :, cols], dst_ref=dst.at[my, gr, :, cols],
                        send_sem=ysnd_r.at[kind, gr, hf, d], recv_sem=yrcv_r.at[kind, gr, hf, my],
                        device_id={"dp": to}, device_id_type=MESH,
                    ).wait_send()
    for kind in range(3):
        for i in range(2):
            pltpu.make_async_remote_copy(
                src_ref=h.at[kind, my], dst_ref=h.at[kind, my],
                send_sem=ysnd_h.at[kind, i], recv_sem=yrcv_h.at[kind, i],
                device_id={"dp": sides[i]}, device_id_type=MESH,
            ).wait_send()
            pltpu.make_async_remote_copy(
                src_ref=h.at[kind, my, i], dst_ref=h.at[kind, my, i],
                send_sem=ysnd_f.at[kind, i], recv_sem=yrcv_f.at[kind, i],
                device_id={"dp": sides[i]}, device_id_type=MESH,
            ).wait_send()
    out_d.wait()
    out_g.wait()
    out_u.wait()


def hand_out(*refs):
    count = (len(refs) - 1) // 3
    srcs, dsts, held, sem = refs[:count], refs[count : 2 * count], refs[2 * count : 3 * count], refs[-1]
    inward = [pltpu.make_async_copy(srcs[i], held[i], sem.at[0, i]) for i in range(count)]
    outward = [pltpu.make_async_copy(held[i], dsts[i], sem.at[1, i]) for i in range(count)]
    for copy in inward:
        copy.start()
    for i in range(count):
        inward[i].wait()
        outward[i].start()
    for copy in outward:
        copy.wait()


def shards(n_e, n_dp, tokens, routes, probs, cotangent, w_gate, w_up, w_down):
    t_n, width = tokens.shape
    top = routes.shape[1]
    el, _, hid = w_gate.shape
    chunk = width // n_dp
    blocks = n_dp * el
    msg = blocks * CAP
    groups = n_e // blocks
    grows = blocks * msg
    slots = n_e * msg
    gb = 4 * msg
    i = np.arange(slots)
    m = i % msg
    local, seat, part = (m % (el * CAP)) // CAP, i % CAP, m // (el * CAP)
    col = np.zeros((gb, 4), np.int32)
    col[:, 0] = ((i // msg) * el + local)[:gb]
    col[:, 1], col[:, 2] = seat[:gb], part[:gb]
    row = np.zeros((8, slots), np.int32)
    row[0], row[1], row[2] = (i // msg) * el + local, seat, part
    j = np.arange(grows)
    perm = (((j % msg) // CAP) * msg + (j // msg) * CAP + j % CAP).astype(np.int32)[:, None]
    vmem = pl.BlockSpec(memory_space=pltpu.VMEM)
    hbm = pl.BlockSpec(memory_space=pl.ANY)
    dma = pltpu.SemaphoreType.DMA
    grad = jax.ShapeDtypeStruct((el, chunk, hid), BF)
    V = pltpu.VMEM
    results = pl.pallas_call(
        functools.partial(layer_kernel, n_e, n_dp),
        out_shape=(
            jax.ShapeDtypeStruct((t_n, width), BF),
            jax.ShapeDtypeStruct((t_n, width), BF),
            jax.ShapeDtypeStruct(probs.shape[::-1], F32),
            grad, grad, grad,
        ),
        in_specs=[hbm] * 10,
        out_specs=[vmem] * 3 + [hbm] * 3,
        scratch_shapes=[V((slots, chunk), BF)] * 6
        + [V((groups, n_dp, el * msg, chunk), BF)] * 2
        + [V((grows, grows), BF), V((slots, n_dp * t_n), BF)]
        + [V((n_dp * t_n, slots), BF)] * 3
        + [V(w_gate.shape, BF)] * 3
        + [V((3, n_dp, groups, el * msg, hid), BF)]
        + [V((n_dp, groups, el * msg, chunk), BF)] * 2
        + [V((el, groups * msg, hid), F32)] * 2
        + [V(tokens.shape, BF)] * 2
        + [V((top, t_n), jnp.int32), V((top, t_n), F32)]
        + [V(a.shape, jnp.int32) for a in (col, row, perm)]
        + [dma((7,)), dma((3,)), dma((4, 4)), dma((3,)), dma((4, 4, n_e)), dma((4, 4, n_e)),
           dma((2, groups, 4, n_dp)), dma((2, groups, 4, n_dp))] + [dma((3, 2))] * 4,
        compiler_params=pltpu.CompilerParams(collective_id=0, has_side_effects=True, vmem_limit_bytes=67043328),
    )(tokens, cotangent, routes.T, probs.T, jnp.asarray(col), jnp.asarray(row), jnp.asarray(perm), w_gate, w_up, w_down)
    shapes = [jax.ShapeDtypeStruct(r.shape, r.dtype) for r in results]
    count = len(shapes)
    mixed, tgrad, pgrad, *grads = pl.pallas_call(
        hand_out,
        out_shape=shapes,
        in_specs=[hbm] * count,
        out_specs=[hbm] * count,
        scratch_shapes=[V(r.shape, r.dtype) for r in shapes] + [dma((2, count))],
    )(*results)
    return mixed, tgrad, pgrad.T, *grads


def solution(mesh):
    both = P(("expert", "dp"), None)
    return jax.shard_map(
        functools.partial(shards, mesh.shape["expert"], mesh.shape["dp"]),
        mesh=mesh,
        in_specs=(both, both, both, both) + (P("expert", None, None),) * 3,
        out_specs=(both, both, both) + (P("expert", "dp", None),) * 3,
        check_vma=False,
    )
```

```python
import functools

import jax
import jax.numpy as jnp
import numpy as np
from jax import lax
from jax.experimental import pallas as pl
from jax.experimental.pallas import tpu as pltpu
from jax.sharding import PartitionSpec as P

MESH = pl.DeviceIdType.MESH
CAP = 5
BF = jnp.bfloat16
F32 = jnp.float32
NT = (((1,), (1,)), ((), ()))
TN = (((0,), (0,)), ((), ()))


def mm(a, b, dims=None, precision=None):
    dims = (((1,), (0,)), ((), ())) if dims is None else dims
    return lax.dot_general(a, b, dims, preferred_element_type=F32, precision=precision)


def layer_kernel(
    n_e, n_dp,
    tok_in, cot_in, routes_in, probs_in, col_in, row_in, perm_in, wg_hbm, wu_hbm, wd_hbm,
    mixed_ref, tgrad_ref, pgrad_ref, gg_hbm, gu_hbm, gd_hbm,
    sa, sb, ra, rb, ro, rd, x, u, q, g, gt, whi, wlo, wg, wu, wd, h, xs, us, pre_g, pre_u,
    tok_ref, cot_ref, routes_ref, probs_ref, col_ref, row_ref, perm_ref,
    in_sem, w_sem, loc_sem, out_sem, snd, rcv, ysnd_r, yrcv_r, y_loc, ysnd_h, yrcv_h, ysnd_f, yrcv_f,
):
    me = lax.axis_index("expert")
    my = lax.axis_index("dp")
    el = wg.shape[0]
    width = tok_ref.shape[1]
    chunk = width // n_dp
    t_n = tok_ref.shape[0]
    top = routes_ref.shape[0]
    n_x = n_e * el
    blocks = n_dp * el
    msg = blocks * CAP
    groups = n_e // blocks
    grows = blocks * msg
    per = blocks * CAP
    gd = 4
    gb = gd * msg

    barrier = pltpu.get_barrier_semaphore()

    @pl.loop(1, n_e)
    def _(d):
        pl.semaphore_signal(barrier, inc=1, device_id={"expert": lax.rem(me + d, n_e)}, device_id_type=MESH)

    for d in range(1, n_dp):
        pl.semaphore_signal(barrier, inc=1, device_id={"dp": lax.rem(my + d, n_dp)}, device_id_type=MESH)

    in_copies = [
        pltpu.make_async_copy(src, dst, in_sem.at[i])
        for i, (src, dst) in enumerate((
            (routes_in, routes_ref), (probs_in, probs_ref), (col_in, col_ref), (tok_in, tok_ref),
            (cot_in, cot_ref), (row_in, row_ref), (perm_in, perm_ref),
        ))
    ]
    w_copies = [
        pltpu.make_async_copy(src, dst, w_sem.at[i])
        for i, (src, dst) in enumerate(((wg_hbm, wg), (wu_hbm, wu), (wd_hbm, wd)))
    ]
    for copy in in_copies[:4]:
        copy.start()
    for copy in in_copies[:4]:
        copy.wait()
    for copy in in_copies[4:] + w_copies:
        copy.start()

    def eye(n):
        return jnp.where(
            lax.broadcasted_iota(jnp.int32, (n, n), 0) == lax.broadcasted_iota(jnp.int32, (n, n), 1), 1.0, 0.0
        )

    exact = lax.Precision.HIGHEST
    routes = mm(routes_ref[...].astype(F32), eye(top), TN, exact)
    probs = mm(probs_ref[...], eye(top), TN, exact)
    totals = jnp.sum(probs, axis=1, keepdims=True)
    share = probs / totals
    lane_x = lax.broadcasted_iota(jnp.int32, (t_n, n_x), 1)
    lane_f = lane_x.astype(F32)
    named = jnp.zeros((t_n, n_x), F32)
    share_x = jnp.zeros((t_n, n_x), F32)
    for j in range(top):
        hit = routes[:, j : j + 1] == lane_f
        named = named + jnp.where(hit, 1.0, 0.0)
        share_x = share_x + jnp.where(hit, share[:, j : j + 1], 0.0)
    before = jnp.where(
        lax.broadcasted_iota(jnp.int32, (t_n, t_n), 0) > lax.broadcasted_iota(jnp.int32, (t_n, t_n), 1), 1.0, 0.0
    ).astype(BF)
    rank = mm(before, named.astype(BF))
    place = jnp.where(named > 0.0, rank, -1.0).astype(BF)
    place_c = jnp.concatenate([place] * n_dp, axis=0)
    share_c = jnp.concatenate([share_x] * n_dp, axis=0)
    tok_c = jnp.concatenate([tok_ref[:, c * chunk : (c + 1) * chunk] for c in range(n_dp)], axis=0)

    lane_e = lax.broadcasted_iota(jnp.int32, (gb, n_x), 1)
    lane_c = lax.broadcasted_iota(jnp.int32, (gb, n_dp * t_n), 1) // t_n
    col_e = col_ref[:, 0:1]
    col_s = col_ref[:, 1:2].astype(F32)
    col_c = col_ref[:, 2:3]
    n_g = n_e // gd

    pieces = (4, 2, 2, 2)

    def span(kind, hf):
        wide = chunk // pieces[kind]
        return pl.ds(hf * wide, wide)

    def message(kind, buf, i, hf):
        return buf.at[pl.ds(pl.multiple_of(i * msg, msg), msg), span(kind, hf)]

    def own(buf):
        return buf.at[pl.ds(pl.multiple_of(me * msg, msg), msg)]

    def send(kind, src, dst, o, hf):
        @pl.when(o != me)
        def _():
            pltpu.make_async_remote_copy(
                src_ref=message(kind, src, o, hf), dst_ref=message(kind, dst, me, hf),
                send_sem=snd.at[kind], recv_sem=rcv.at[kind, hf],
                device_id={"expert": o}, device_id_type=MESH,
            ).start()

        if hf == 0:
            @pl.when(o == me)
            def _():
                pltpu.make_async_copy(own(src), own(dst), loc_sem.at[kind]).start()

    def send_all(kind, src, dst, hf):
        @pl.loop(0, 8)
        def _(i):
            k = i // 2
            z = lax.rem(me // 8 + 2 + 3 * k + 3 * (k // 2) + 2 * (k // 3), 4)
            core = lax.rem(me + i, 2)
            for dx in (2, 1, 3, 0):
                send(kind, src, dst, z * 8 + lax.rem(me // 2 + dx, 4) * 2 + core, hf)

    others = (n_e - 1) * msg

    def await_sent(kind, src):
        part = src.at[0:others]
        pltpu.make_async_remote_copy(
            src_ref=part, dst_ref=part, send_sem=snd.at[kind], recv_sem=rcv.at[kind, 0],
            device_id={"dp": my}, device_id_type=MESH,
        ).wait_send()

    def await_all(kind, dst, hf):
        part = dst.at[0:others, span(kind, hf)]
        pltpu.make_async_remote_copy(
            src_ref=part, dst_ref=part, send_sem=snd.at[kind], recv_sem=rcv.at[kind, hf],
            device_id={"dp": my}, device_id_type=MESH,
        ).wait_recv()
        if hf == 0:
            pltpu.make_async_copy(own(dst), own(dst), loc_sem.at[kind]).wait()

    def pick(og):
        return jnp.where(lane_e == col_e + og * (gd * el), 1.0, 0.0)

    pl.semaphore_wait(barrier, n_e - 1 + n_dp - 1)

    @pl.loop(0, n_g)
    def _(i):
        og = lax.rem(me // gd + 5 * i + 5, n_g)
        rows = pl.ds(pl.multiple_of(og * gb, gb), gb)
        held = mm(pick(og).astype(BF), place_c, NT)
        chosen = jnp.where((held == col_s) & (lane_c == col_c), 1.0, 0.0).astype(BF)
        g[rows, :] = chosen
        sa[rows, :] = mm(chosen, tok_c).astype(BF)
        for k in range(gd):
            send(0, sa, ra, og * gd + k, 0)

    for hf in range(1, pieces[0]):
        send_all(0, sa, ra, hf)

    for copy in in_copies[4:]:
        copy.wait()
    cot_c = jnp.concatenate([cot_ref[:, c * chunk : (c + 1) * chunk] for c in range(n_dp)], axis=0)

    @pl.loop(0, n_g)
    def _(i):
        og = lax.rem(me // gd + 5 * i + 5, n_g)
        rows = pl.ds(pl.multiple_of(og * gb, gb), gb)
        chosen = g[rows, :]
        scale = mm(pick(og), share_c, NT, lax.Precision.HIGHEST)
        scale = jnp.sum(scale * chosen.astype(F32), axis=1, keepdims=True)
        sb[rows, :] = (mm(chosen, cot_c) * scale).astype(BF)

    send_all(1, sb, rb, 0)
    send_all(1, sb, rb, 1)

    half = grows // 2
    for p in range(2):
        q[p * half : (p + 1) * half, :] = jnp.where(
            lax.broadcasted_iota(jnp.int32, (half, grows), 1) == perm_ref[p * half : (p + 1) * half, 0:1], 1.0, 0.0
        ).astype(BF)
    tcols = n_e * msg // 4
    sub_e = lax.broadcasted_iota(jnp.int32, (n_x, tcols), 0)
    sub_c = lax.broadcasted_iota(jnp.int32, (n_dp * t_n, tcols), 0) // t_n
    for p in range(4):
        cols = slice(p * tcols, (p + 1) * tcols)
        pick_t = jnp.where(sub_e == row_ref[0:1, cols], 1.0, 0.0)
        held = mm(place_c, pick_t.astype(BF))
        here = (held == row_ref[1:2, cols].astype(F32)) & (sub_c == row_ref[2:3, cols])
        gt[:, cols] = jnp.where(here, 1.0, 0.0).astype(BF)
        weight = jnp.where(here, mm(share_c, pick_t, None, lax.Precision.HIGHEST), 0.0)
        high = weight.astype(BF)
        whi[:, cols] = high
        wlo[:, cols] = (weight - high.astype(F32)).astype(BF)

    def regroup(dst_write, src, gr, cols):
        for p in range(2):
            dst_write(p, mm(q[p * half : (p + 1) * half, :], src[gr * grows : (gr + 1) * grows, cols]).astype(BF))

    ex_rows = el * per

    def y_rows(kind, src, dst, gr, hf):
        cols = span(kind, hf)
        for d in (1, n_dp - 1, 2):
            to = lax.rem(my + d, n_dp)
            pltpu.make_async_remote_copy(
                src_ref=src.at[gr, to, :, cols], dst_ref=dst.at[my, gr, :, cols],
                send_sem=ysnd_r.at[kind], recv_sem=yrcv_r.at[kind],
                device_id={"dp": to}, device_id_type=MESH,
            ).start()
        pltpu.make_async_copy(src.at[gr, my, :, cols], dst.at[my, gr, :, cols], y_loc.at[kind]).start()

    def y_rows_done(kind, dst):
        part = dst.at[0 : n_dp - 1]
        return pltpu.make_async_remote_copy(
            src_ref=part, dst_ref=part, send_sem=ysnd_r.at[kind], recv_sem=yrcv_r.at[kind],
            device_id={"expert": me}, device_id_type=MESH,
        )

    def y_rows_wait(kind, dst):
        y_rows_done(kind, dst).wait_recv()
        pltpu.make_async_copy(dst.at[my], dst.at[my], y_loc.at[kind]).wait()

    far = lax.rem(my + 2, n_dp)
    sides = (lax.rem(my + 1, n_dp), lax.rem(my + n_dp - 1, n_dp))

    def y_hidden(kind):
        for i in range(2):
            pltpu.make_async_remote_copy(
                src_ref=h.at[kind, my], dst_ref=h.at[kind, my],
                send_sem=ysnd_h.at[kind, i], recv_sem=yrcv_h.at[kind, i],
                device_id={"dp": sides[i]}, device_id_type=MESH,
            ).start()

    def hand_on(kind, i):
        held = sides[1 - i]
        pltpu.make_async_remote_copy(
            src_ref=h.at[kind, held], dst_ref=h.at[kind, held],
            send_sem=ysnd_h.at[kind, i], recv_sem=yrcv_h.at[kind, i],
            device_id={"dp": held}, device_id_type=MESH,
        ).wait_recv()
        pltpu.make_async_remote_copy(
            src_ref=h.at[kind, held, i], dst_ref=h.at[kind, held, i],
            send_sem=ysnd_f.at[kind, i], recv_sem=yrcv_f.at[kind, i],
            device_id={"dp": sides[i]}, device_id_type=MESH,
        ).start()

    def y_hidden_far(kind):
        for i in range(2):
            pltpu.make_async_remote_copy(
                src_ref=h.at[kind, far, i], dst_ref=h.at[kind, far, i],
                send_sem=ysnd_f.at[kind, i], recv_sem=yrcv_f.at[kind, i],
                device_id={"dp": sides[i]}, device_id_type=MESH,
            ).wait_recv()

    def into(dst, gr, cols):
        def write(p, value):
            for c in range(n_dp // 2):
                dst[gr, p * (n_dp // 2) + c, :, cols] = value[c * ex_rows : (c + 1) * ex_rows]
        return write

    for hf in range(pieces[0]):
        await_all(0, ra, hf)
        for gr in range(groups):
            regroup(into(x, gr, span(0, hf)), ra, gr, span(0, hf))
            y_rows(0, x, xs, gr, hf)

    def rows_of(src, c, e):
        return jnp.concatenate([src[gr, c, pl.ds(pl.multiple_of(e * per, per), per), :] for gr in range(groups)], axis=0)

    def keep_hidden(kind, e, value):
        for gr in range(groups):
            h[kind, my, gr, pl.ds(pl.multiple_of(e * per, per), per), :] = value[gr * per : (gr + 1) * per]

    def keep_rows(dst, c, e, value):
        for gr in range(groups):
            dst[pl.ds(pl.multiple_of(gr * grows + (c * el + e) * per, per), per), :] = value[gr * per : (gr + 1) * per]

    w_copies[0].wait()
    w_copies[1].wait()
    w_copies[2].wait()

    @pl.loop(0, el)
    def _(e):
        gate = 0.0
        up = 0.0
        for c in range(n_dp):
            rows = rows_of(x, c, e)
            gate = gate + mm(rows, wg[e, c * chunk : (c + 1) * chunk, :])
            up = up + mm(rows, wu[e, c * chunk : (c + 1) * chunk, :])
        pre_g[e] = gate
        pre_u[e] = up
        active = (gate * jax.nn.sigmoid(gate) * up).astype(BF)
        keep_hidden(0, e, active)
        for c in range(n_dp):
            keep_rows(ra, c, e, mm(active, wd[e, c * chunk : (c + 1) * chunk, :], NT).astype(BF))

    y_hidden(0)
    await_sent(0, sa)

    def plain(dst, gr):
        def write(p, value):
            dst[gr * grows + p * half : gr * grows + (p + 1) * half, :] = value
        return write

    for gr in range(groups):
        regroup(plain(sa, gr), ra, gr, slice(0, chunk))
    for hf in range(pieces[2]):
        send_all(2, sa, ro, hf)

    for hf in range(pieces[1]):
        await_all(1, rb, hf)
        for gr in range(groups):
            regroup(into(u, gr, span(1, hf)), rb, gr, span(1, hf))
        if hf == 0:
            hand_on(0, 0)
            hand_on(0, 1)
        for gr in range(groups):
            y_rows(1, u, us, gr, hf)

    @pl.loop(0, el)
    def _(e):
        d_active = 0.0
        for c in range(n_dp):
            d_active = d_active + mm(rows_of(u, c, e), wd[e, c * chunk : (c + 1) * chunk, :])
        gate = pre_g[e]
        up = pre_u[e]
        sig = jax.nn.sigmoid(gate)
        d_gate = (d_active * up * sig * (1.0 + gate * (1.0 - sig))).astype(BF)
        d_up = (d_active * gate * sig).astype(BF)
        keep_hidden(1, e, d_gate)
        keep_hidden(2, e, d_up)
        for c in range(n_dp):
            cols = slice(c * chunk, (c + 1) * chunk)
            keep_rows(rb, c, e, (mm(d_gate, wg[e, cols, :], NT) + mm(d_up, wu[e, cols, :], NT)).astype(BF))

    y_hidden(1)
    y_hidden(2)
    await_sent(1, sb)
    for gr in range(groups):
        regroup(plain(sb, gr), rb, gr, slice(0, chunk))
    for hf in range(pieces[3]):
        send_all(3, sb, rd, hf)

    for hf in range(pieces[2]):
        await_all(2, ro, hf)
    mixed = mm(whi[...], ro[...]) + mm(wlo[...], ro[...])
    for c in range(n_dp):
        mixed_ref[:, c * chunk : (c + 1) * chunk] = mixed[c * t_n : (c + 1) * t_n].astype(BF)
    grad_x = jnp.zeros((n_dp * t_n, n_x), F32)
    for og in range(n_g):
        rows = slice(og * gb, (og + 1) * gb)
        dots = jnp.sum(mm(g[rows, :], cot_c) * ro[rows, :].astype(F32), axis=1, keepdims=True)
        spread = pick(og) * dots
        high = spread.astype(BF)
        low = (spread - high.astype(F32)).astype(BF)
        grad_x = grad_x + mm(gt[:, rows], high) + mm(gt[:, rows], low)
    share_grad_x = grad_x[0:t_n]
    for c in range(1, n_dp):
        share_grad_x = share_grad_x + grad_x[c * t_n : (c + 1) * t_n]
    inner = jnp.sum(share_grad_x * share_x, axis=1, keepdims=True)
    grads = []
    for j in range(top):
        mine = jnp.sum(jnp.where(routes[:, j : j + 1] == lane_f, share_grad_x, 0.0), axis=1, keepdims=True)
        grads.append((mine - inner) / totals)
    lane_j = lax.broadcasted_iota(jnp.int32, (t_n, top), 1)
    prob_grad = jnp.zeros((t_n, top), F32)
    for j in range(top):
        prob_grad = jnp.where(lane_j == j, grads[j], prob_grad)
    pgrad_ref[...] = mm(prob_grad, eye(t_n), TN, exact)

    def gathered(src, e):
        return jnp.concatenate(
            [src[r, gr, pl.ds(pl.multiple_of(e * per, per), per), :] for r in range(n_dp) for gr in range(groups)], axis=0
        )

    def hidden_of(kind, e):
        return jnp.concatenate(
            [h[kind, r, gr, pl.ds(pl.multiple_of(e * per, per), per), :] for r in range(n_dp) for gr in range(groups)],
            axis=0,
        )

    y_hidden_far(0)
    y_rows_wait(0, xs)
    y_rows_wait(1, us)

    @pl.loop(0, el)
    def _(e):
        wg[e, 2 * chunk : 3 * chunk, :] = mm(gathered(us, e), hidden_of(0, e), TN).astype(BF)

    out_d = pltpu.make_async_copy(wg.at[:, 2 * chunk : 3 * chunk], gd_hbm, out_sem.at[2])
    out_d.start()

    for kind in (1, 2):
        hand_on(kind, 0)
        hand_on(kind, 1)

    y_hidden_far(1)

    @pl.loop(0, el)
    def _(e):
        wg[e, 0 * chunk : 1 * chunk, :] = mm(gathered(xs, e), hidden_of(1, e), TN).astype(BF)

    out_g = pltpu.make_async_copy(wg.at[:, 0 * chunk : 1 * chunk], gg_hbm, out_sem.at[0])
    out_g.start()
    y_hidden_far(2)

    @pl.loop(0, el)
    def _(e):
        wg[e, 1 * chunk : 2 * chunk, :] = mm(gathered(xs, e), hidden_of(2, e), TN).astype(BF)

    out_u = pltpu.make_async_copy(wg.at[:, 1 * chunk : 2 * chunk], gu_hbm, out_sem.at[1])
    out_u.start()

    for hf in range(pieces[3]):
        await_all(3, rd, hf)
    tgrad = mm(gt[...], rd[...])
    for c in range(n_dp):
        tgrad_ref[:, c * chunk : (c + 1) * chunk] = tgrad[c * t_n : (c + 1) * t_n].astype(BF)

    await_sent(2, sa)
    await_sent(3, sb)
    y_rows_done(0, xs).wait_send()
    y_rows_done(1, us).wait_send()
    for kind in range(3):
        for i in range(2):
            pltpu.make_async_remote_copy(
                src_ref=h.at[kind, my], dst_ref=h.at[kind, my],
                send_sem=ysnd_h.at[kind, i], recv_sem=yrcv_h.at[kind, i],
                device_id={"dp": sides[i]}, device_id_type=MESH,
            ).wait_send()
            pltpu.make_async_remote_copy(
                src_ref=h.at[kind, my, i], dst_ref=h.at[kind, my, i],
                send_sem=ysnd_f.at[kind, i], recv_sem=yrcv_f.at[kind, i],
                device_id={"dp": sides[i]}, device_id_type=MESH,
            ).wait_send()
    out_d.wait()
    out_g.wait()
    out_u.wait()


def hand_out(*refs):
    count = (len(refs) - 1) // 3
    srcs, dsts, held, sem = refs[:count], refs[count : 2 * count], refs[2 * count : 3 * count], refs[-1]
    inward, outward = [], []
    for i in list(range(3, count)) + [0, 1, 2]:
        for at in (range(srcs[i].shape[0]) if i > 2 else [slice(None)]):
            n = len(inward)
            inward.append(pltpu.make_async_copy(srcs[i].at[at], held[i].at[at], sem.at[0, n]))
            outward.append(pltpu.make_async_copy(held[i].at[at], dsts[i].at[at], sem.at[1, n]))
    for copy in inward:
        copy.start()
    for into, out in zip(inward, outward):
        into.wait()
        out.start()
    for copy in outward:
        copy.wait()


def shards(n_e, n_dp, tokens, routes, probs, cotangent, w_gate, w_up, w_down):
    t_n, width = tokens.shape
    top = routes.shape[1]
    el, _, hid = w_gate.shape
    chunk = width // n_dp
    blocks = n_dp * el
    msg = blocks * CAP
    groups = n_e // blocks
    grows = blocks * msg
    slots = n_e * msg
    gb = 4 * msg
    i = np.arange(slots)
    m = i % msg
    local, seat, part = (m % (el * CAP)) // CAP, i % CAP, m // (el * CAP)
    col = np.zeros((gb, 4), np.int32)
    col[:, 0] = ((i // msg) * el + local)[:gb]
    col[:, 1], col[:, 2] = seat[:gb], part[:gb]
    row = np.zeros((8, slots), np.int32)
    row[0], row[1], row[2] = (i // msg) * el + local, seat, part
    j = np.arange(grows)
    perm = (((j % msg) // CAP) * msg + (j // msg) * CAP + j % CAP).astype(np.int32)[:, None]
    vmem = pl.BlockSpec(memory_space=pltpu.VMEM)
    hbm = pl.BlockSpec(memory_space=pl.ANY)
    dma = pltpu.SemaphoreType.DMA
    grad = jax.ShapeDtypeStruct((el, chunk, hid), BF)
    V = pltpu.VMEM
    results = pl.pallas_call(
        functools.partial(layer_kernel, n_e, n_dp),
        out_shape=(
            jax.ShapeDtypeStruct((t_n, width), BF),
            jax.ShapeDtypeStruct((t_n, width), BF),
            jax.ShapeDtypeStruct(probs.shape[::-1], F32),
            grad, grad, grad,
        ),
        in_specs=[hbm] * 10,
        out_specs=[vmem] * 3 + [hbm] * 3,
        scratch_shapes=[V((slots, chunk), BF)] * 6
        + [V((groups, n_dp, el * msg, chunk), BF)] * 2
        + [V((grows, grows), BF), V((slots, n_dp * t_n), BF)]
        + [V((n_dp * t_n, slots), BF)] * 3
        + [V(w_gate.shape, BF)] * 3
        + [V((3, n_dp, groups, el * msg, hid), BF)]
        + [V((n_dp, groups, el * msg, chunk), BF)] * 2
        + [V((el, groups * msg, hid), F32)] * 2
        + [V(tokens.shape, BF)] * 2
        + [V((top, t_n), jnp.int32), V((top, t_n), F32)]
        + [V(a.shape, jnp.int32) for a in (col, row, perm)]
        + [dma((7,)), dma((3,)), dma((4,)), dma((3,)), dma((4,)), dma((4, 4)), dma((2,)), dma((2,)), dma((2,))] + [dma((3, 2))] * 4,
        compiler_params=pltpu.CompilerParams(collective_id=0, has_side_effects=True, vmem_limit_bytes=67043328),
    )(tokens, cotangent, routes.T, probs.T, jnp.asarray(col), jnp.asarray(row), jnp.asarray(perm), w_gate, w_up, w_down)
    shapes = [jax.ShapeDtypeStruct(r.shape, r.dtype) for r in results]
    count = len(shapes)
    mixed, tgrad, pgrad, *grads = pl.pallas_call(
        hand_out,
        out_shape=shapes,
        in_specs=[hbm] * count,
        out_specs=[hbm] * count,
        scratch_shapes=[V(r.shape, r.dtype) for r in shapes] + [dma((2, 3 + 3 * el))],
    )(*results)
    return mixed, tgrad, pgrad.T, *grads


def solution(mesh):
    both = P(("expert", "dp"), None)
    return jax.shard_map(
        functools.partial(shards, mesh.shape["expert"], mesh.shape["dp"]),
        mesh=mesh,
        in_specs=(both, both, both, both) + (P("expert", None, None),) * 3,
        out_specs=(both, both, both) + (P("expert", "dp", None),) * 3,
        check_vma=False,
    )
```
